128 devices in a mesh: seg: 4 (over x), chan: 32 (over z, y, core).
Axes of the slice: x: 4, y: 4, z: 4, core: 2. Of those that a mesh axis runs over, the one named last changes fastest.
Arguments:
- strain_rate: bfloat16 [48, 1024, 4096], P('seg', None, 'chan'), may hold values from -6 to 6
- window_length: int32 [48], P('seg'), may hold values from 1024 to 4096, as said below
- source_channel: int32 [128], replicated, may hold values from 0 to 1023, as said below
Outputs:
- stacked: float32 [1024, 128, 512], P('chan', 'seg')
The draws below stay inside these ranges and needn't reach their ends.
Inputs may be any that keep to these rules, and one draw needn't show every extreme that they name: `window_length`: window 0 is fully recorded and window 1 holds exactly 1024 recorded samples. `source_channel`: the virtual sources are distinct channels; channel 0 and the last channel are always among them.
All inputs are finite; a program needn't handle non-finite values.
Results may differ from the reference program's by a relative error of at most 0.0045.
Values may be sent and summed in bfloat16 or wider, within the bound.
A program may use at most 128 MiB of HBM per device.

```python
import math
import jax
import jax.numpy as jnp
from jax import lax

W = 4096
NF = 1152
FIRST_BIN = 16
SMOOTH = 64
MAXLAG = 256
VS = 128
SEGWIN = 12
CH_DEV = 32
LAGS = 512
CHANNELS = 1024
WINDOWS = 48
N_SEG = 4


def draw_window_length(key, part):
    lengths = jax.random.randint(jax.random.fold_in(key, 11), (N_SEG * SEGWIN,), W // 4, W + 1)
    lengths = lengths.at[0].set(W)
    lengths = lengths.at[1].set(W // 4)
    return lengths.astype(jnp.int32)


def draw_source_channel(key, part):
    inner = jax.random.permutation(jax.random.fold_in(key, 21), CHANNELS - 2)[:VS - 2] + 1
    picked = jnp.concatenate([jnp.zeros((1,), jnp.int32), jnp.full((1,), CHANNELS - 1, jnp.int32), inner.astype(jnp.int32)])
    order = jax.random.permutation(jax.random.fold_in(key, 22), VS)
    return picked[order].astype(jnp.int32)


def block_scale(own_key, extent, cuts, smallest, top_value):
    loudness, own = 1.0, jax.random.fold_in(own_key, 6)
    for axis_at, parts in cuts:
        heights = jnp.exp(jax.random.uniform(jax.random.fold_in(own, axis_at), (parts,), jnp.float32, smallest / len(cuts), top_value / len(cuts)))
        loudness = loudness * jnp.repeat(heights, extent[axis_at] // parts).reshape([-1 if axis == axis_at else 1 for axis in range(len(extent))])
    return loudness


def centred(stream_key, dims, deviation, limit, shards=(), kind=jnp.bfloat16):
    drawn = deviation * jax.random.normal(stream_key, dims, jnp.float32)
    if shards:
        drawn = drawn * block_scale(stream_key, dims, shards, -0.22, 0.18)
    return jnp.clip(drawn, -limit, limit).astype(kind)


def setup_inputs(seed: int = 0) -> dict:
    key_of = jax.random.split(jax.random.key(seed), 4)
    strain_rate = centred(key_of[0], (WINDOWS, CHANNELS, W), 1.0, 6.0, ((0, 4), (2, 32)))
    window_length = draw_window_length(jax.random.fold_in(key_of[3], 71), 0)
    source_channel = draw_source_channel(jax.random.fold_in(key_of[3], 71), 0)
    return dict(strain_rate=strain_rate, window_length=window_length, source_channel=source_channel)


def angles(first, second):
    product = jnp.mod(first[:, None] * second[None, :], W)
    return product.astype(jnp.float32) * (2.0 * math.pi / W)

def forward_table():
    samples = jnp.arange(W, dtype=jnp.int32)
    freqs = FIRST_BIN + jnp.arange(NF, dtype=jnp.int32)
    phase = angles(samples, freqs)
    return jnp.concatenate([jnp.cos(phase), -jnp.sin(phase)], axis=1).astype(jnp.bfloat16)

def inverse_table():
    freqs = FIRST_BIN + jnp.arange(NF, dtype=jnp.int32)
    shifts = jnp.arange(LAGS, dtype=jnp.int32) - MAXLAG
    phase = angles(freqs, shifts)
    return jnp.concatenate([jnp.cos(phase), -jnp.sin(phase)], axis=0).astype(jnp.bfloat16)

def band_matrix():
    offsets = jnp.arange(NF, dtype=jnp.int32)
    nearby = jnp.abs(offsets[:, None] - offsets[None, :]) <= SMOOTH
    return (nearby.astype(jnp.bfloat16), lax.optimization_barrier(jnp.sum(nearby.astype(jnp.float32), axis=0)))

def whiten(signal, table, nearby, counts):
    spectrum = jnp.dot(signal, table, preferred_element_type=jnp.float32)
    spec_real = spectrum[:, :NF]
    spec_imag = spectrum[:, NF:]
    magnitude = jnp.sqrt(spec_real * spec_real + spec_imag * spec_imag).astype(jnp.bfloat16)
    smooth = jnp.dot(magnitude, nearby, preferred_element_type=jnp.float32) / counts + 1e-06
    return ((spec_real / smooth).astype(jnp.bfloat16), (spec_imag / smooth).astype(jnp.bfloat16))

def reference(strain_rate, window_length, source_channel):
    sample_index = jnp.arange(W, dtype=jnp.int32)
    inside = sample_index[None, :] < window_length[:, None]
    masked = jnp.where(inside[:, None, :], strain_rate, jnp.zeros((), jnp.bfloat16))
    grouped = masked.reshape(N_SEG, SEGWIN, CHANNELS, W)
    table = forward_table()
    lag_table = inverse_table()
    nearby, counts = band_matrix()

    def segment(carry, block):
        white_real, white_imag = whiten(block.reshape(SEGWIN * CHANNELS, W), table, nearby, counts)
        white_real = white_real.reshape(SEGWIN, CHANNELS, NF)
        white_imag = white_imag.reshape(SEGWIN, CHANNELS, NF)
        source_real = white_real[:, source_channel, :].astype(jnp.float32)
        source_imag = white_imag[:, source_channel, :].astype(jnp.float32)

        def correlate(start):
            part_real = lax.dynamic_slice_in_dim(white_real, start, CH_DEV, 1).astype(jnp.float32)
            part_imag = lax.dynamic_slice_in_dim(white_imag, start, CH_DEV, 1).astype(jnp.float32)
            cross_real = jnp.einsum('wck,wsk->csk', part_real, source_real) + jnp.einsum('wck,wsk->csk', part_imag, source_imag)
            cross_imag = jnp.einsum('wck,wsk->csk', part_imag, source_real) - jnp.einsum('wck,wsk->csk', part_real, source_imag)
            joined = jnp.concatenate([cross_real, cross_imag], axis=-1).astype(jnp.bfloat16)
            joined = joined.reshape(CH_DEV * VS, 2 * NF)
            return jnp.dot(joined, lag_table, preferred_element_type=jnp.float32).reshape(CH_DEV, VS, LAGS)
        starts = jnp.arange(CHANNELS // CH_DEV, dtype=jnp.int32) * CH_DEV
        blocks = lax.map(correlate, starts)
        return (carry + blocks.reshape(CHANNELS, VS, LAGS), None)
    summed, _ = lax.scan(segment, jnp.zeros((CHANNELS, VS, LAGS), jnp.float32), grouped)
    return summed * (1.0 / math.sqrt(NF * SEGWIN * N_SEG))
```

```python
import math

import jax
import jax.numpy as jnp
import numpy as np
from jax import lax
from jax.experimental import pallas as pl
from jax.experimental.pallas import tpu as pltpu
from jax.sharding import PartitionSpec as P

W = 4096
NF = 1152
FIRST_BIN = 16
SMOOTH = 64
MAXLAG = 256
LAGS = 512
VS = 128
CHAN = 32
SEG = 4
WIN = 12
CH = 32
NKB = NF // 128
ROWS_MAIN = WIN * CH
ROWS_SRC = 48
ROWS = ROWS_MAIN + ROWS_SRC
MESH = pl.DeviceIdType.MESH
BF = jnp.bfloat16
F32 = jnp.float32


def unit(product):
    phase = np.mod(product, W).astype(np.float64) * (2.0 * math.pi / W)
    return np.cos(phase).astype(np.float32), np.sin(phase).astype(np.float32)


def small_tables():
    freqs = FIRST_BIN + np.arange(NF)
    coarse = unit(64 * np.arange(64)[:, None] * freqs[None, :128])
    fine = unit(np.arange(64)[:, None] * freqs[None, :])
    lag_coarse = unit(64 * (np.arange(8)[:, None] - 4) * freqs[None, :128])
    width = np.abs(np.arange(NF)[:, None] - np.arange(NF)[None, :]) <= SMOOTH
    inverse = (1.0 / width.sum(axis=0)).astype(np.float32).reshape(1, NF)
    return coarse, fine, lag_coarse, inverse


def slot_masks(rows):
    lane = lax.broadcasted_iota(jnp.int32, (rows, 128), 1)
    return [((lane // 8) // (1 << b)) % 2 == 1 for b in range(4)]


def interleave(values, masks):
    zero = jnp.zeros_like(values[0])
    state = [pltpu.roll(v, 8 * w, 1) if w else v for w, v in enumerate(values)]
    state = state + [zero] * (16 - len(state))
    for b in range(4):
        state = [
            jnp.where(masks[b], state[(i + (1 << b)) % 16], state[i]) for i in range(16)
        ]
    return [state[(-m) % 16] for m in range(16)]


def spectra_kernel(
    x_ref, wl_ref, sc_ref, ca_ref, sa_ref, cb_ref, sb_ref, inv_ref,
    a_out, b_out,
    xv, xs, rm, rs, tab, lhs, acc, magp,
    ssem, rsem, ssem2, rsem2, lsem,
):
    me = lax.axis_index("chan")
    core = lax.rem(me, 2)
    load = pltpu.make_async_copy(x_ref, xv, lsem.at[0])
    load.start()
    barrier = pltpu.get_barrier_semaphore()

    def greet(d, _):
        pl.semaphore_signal(
            barrier, inc=1, device_id={"chan": lax.rem(me + d, CHAN)}, device_id_type=MESH
        )
        return 0

    lax.fori_loop(1, CHAN, greet, 0)
    pl.semaphore_wait(barrier, CHAN - 1)

    def main_copy(d, source):
        peer = lax.rem(me + d, CHAN)
        return pltpu.make_async_remote_copy(
            src_ref=x_ref.at[:, pl.ds(peer * CH, CH), :],
            dst_ref=rm.at[source],
            send_sem=ssem.at[d],
            recv_sem=rsem.at[source],
            device_id={"chan": peer},
            device_id_type=MESH,
        )

    def src_copy(d, source):
        peer = lax.rem(me + d, CHAN)
        return pltpu.make_async_remote_copy(
            src_ref=xs.at[peer],
            dst_ref=rs.at[source],
            send_sem=ssem2.at[d],
            recv_sem=rsem2.at[source],
            device_id={"chan": peer},
            device_id_type=MESH,
        )

    def send(d, _):
        main_copy(d, me).start()
        return 0

    lax.fori_loop(1, CHAN, send, 0)
    own = pltpu.make_async_copy(x_ref.at[:, pl.ds(me * CH, CH), :], rm.at[me], lsem.at[1])
    own.start()

    load.wait()
    hot = (
        lax.broadcasted_iota(jnp.int32, (VS, CHAN * CH), 1) == sc_ref[...]
    ).astype(F32).astype(BF)

    def pick(pair, _):
        first = jnp.dot(hot, xv[2 * pair], preferred_element_type=F32)
        second = jnp.dot(hot, xv[2 * pair + 1], preferred_element_type=F32)
        half = pair // 3
        row = pl.multiple_of(lax.rem(pair, 3) * 16, 16)
        for q in range(16):
            both = jnp.concatenate([first[8 * q:8 * q + 8], second[8 * q:8 * q + 8]], axis=0)
            xs[2 * q + half, pl.ds(row, 16), :] = both.astype(BF)
        return 0

    lax.fori_loop(0, WIN // 2, pick, 0)

    def send_src(d, _):
        src_copy(d, me).start()
        return 0

    lax.fori_loop(1, CHAN, send_src, 0)
    own2 = pltpu.make_async_copy(xs.at[me], rs.at[me], lsem.at[2])
    own2.start()

    def make_rows(a, _):
        row = pl.multiple_of(a * 64, 64)
        ca = jnp.broadcast_to(ca_ref[pl.ds(a, 1), :], (64, 128))
        sa = jnp.broadcast_to(sa_ref[pl.ds(a, 1), :], (64, 128))
        for kb in range(NKB):
            cb = cb_ref[:, kb * 128:kb * 128 + 128]
            sb = sb_ref[:, kb * 128:kb * 128 + 128]
            tab[pl.ds(row, 64), kb * 128:kb * 128 + 128] = (ca * cb - sa * sb).astype(BF)
            tab[pl.ds(row, 64), NF + kb * 128:NF + kb * 128 + 128] = (
                -(sa * cb + ca * sb)
            ).astype(BF)
        return 0

    lax.fori_loop(0, 64, make_rows, 0)
    acc[...] = jnp.zeros_like(acc)
    own.wait()
    own2.wait()

    lane = lax.broadcasted_iota(jnp.int32, (1, 128), 1)

    def gather_group(step, _):
        group = lax.rem(me // 4 + CHAN // 4 - step, CHAN // 4)
        for i in range(4):
            j = group * 4 + i

            @pl.when(j != me)
            def _():
                main_copy(0, j).wait_recv()
                src_copy(0, j).wait_recv()

            def keep(w):
                inside = lane + j * 128 < wl_ref[w]
                return jnp.where(inside, 1.0, 0.0).astype(BF)

            for w in range(WIN):
                lhs[w * CH:(w + 1) * CH, i * 128:(i + 1) * 128] = rm[j, w] * keep(w)
            for t in range(3):
                upper = jnp.broadcast_to(keep(core * 6 + 2 * t).astype(F32), (8, 128))
                lower = jnp.broadcast_to(keep(core * 6 + 2 * t + 1).astype(F32), (8, 128))
                both = jnp.concatenate([upper, lower], axis=0).astype(BF)
                lhs[ROWS_MAIN + 16 * t:ROWS_MAIN + 16 * t + 16, i * 128:(i + 1) * 128] = (
                    rs[j, 16 * t:16 * t + 16, :] * both
                )

        def column(ct, _):
            col = pl.multiple_of(ct * 256, 256)
            row = pl.multiple_of(group * 512, 512)
            acc[:, pl.ds(col, 256)] += jnp.dot(
                lhs[...], tab[pl.ds(row, 512), pl.ds(col, 256)], preferred_element_type=F32
            )
            return 0

        lax.fori_loop(0, 2 * NF // 256, column, 0)
        return 0

    lax.fori_loop(0, CHAN // 4, gather_group, 0)

    def sent(d, _):
        main_copy(d, me).wait_send()
        src_copy(d, me).wait_send()
        return 0

    lax.fori_loop(1, CHAN, sent, 0)

    magp[:, 0:128] = jnp.zeros((ROWS, 128), BF)
    magp[:, NF + 128:NF + 256] = jnp.zeros((ROWS, 128), BF)

    def magnitude(kb, _):
        col = pl.multiple_of(kb * 128, 128)
        re = acc[:, pl.ds(col, 128)]
        im = acc[:, pl.ds(pl.multiple_of(NF + col, 128), 128)]
        magp[:, pl.ds(pl.multiple_of(col + 128, 128), 128)] = jnp.sqrt(re * re + im * im).astype(BF)
        return 0

    lax.fori_loop(0, NKB, magnitude, 0)
    band = (
        jnp.abs(
            lax.broadcasted_iota(jnp.int32, (384, 128), 0)
            - 128
            - lax.broadcasted_iota(jnp.int32, (384, 128), 1)
        )
        <= SMOOTH
    ).astype(F32).astype(BF)

    def whiten(kb, _):
        col = pl.multiple_of(kb * 128, 128)
        col2 = pl.multiple_of(NF + col, 128)
        total = jnp.dot(magp[:, pl.ds(col, 384)], band, preferred_element_type=F32)
        scale = 1.0 / (total * inv_ref[:, pl.ds(col, 128)] + 1e-06)
        acc[:, pl.ds(col, 128)] = acc[:, pl.ds(col, 128)] * scale
        acc[:, pl.ds(col2, 128)] = acc[:, pl.ds(col2, 128)] * scale
        return 0

    lax.fori_loop(0, NKB, whiten, 0)

    b_out[...] = acc[ROWS_MAIN:, :].astype(BF)
    masks = slot_masks(8)

    def spread(step, _):
        kb = step // 4
        c8 = pl.multiple_of(lax.rem(step, 4) * 8, 8)
        for ri in range(2):
            col = pl.multiple_of(ri * NF + kb * 128, 128)
            values = [
                acc[pl.ds(pl.multiple_of(w * CH + c8, 8), 8), pl.ds(col, 128)] for w in range(WIN)
            ]
            for m, out in enumerate(interleave(values, masks)):
                a_out[kb * 16 + m, ri, pl.ds(c8, 8), :] = out
        return 0

    lax.fori_loop(0, NKB * 4, spread, 0)


def spectra(x, wl, sc, tables):
    (ca, sa), (cb, sb), _, inverse = tables
    vmem = pl.BlockSpec(memory_space=pltpu.VMEM)
    return pl.pallas_call(
        spectra_kernel,
        out_shape=(
            jax.ShapeDtypeStruct((NKB * 16, 2, CH, 128), F32),
            jax.ShapeDtypeStruct((ROWS_SRC, 2 * NF), BF),
        ),
        in_specs=[
            pl.BlockSpec(memory_space=pl.ANY),
            pl.BlockSpec(memory_space=pltpu.SMEM),
            vmem, vmem, vmem, vmem, vmem, vmem,
        ],
        out_specs=(vmem, vmem),
        scratch_shapes=[
            pltpu.VMEM((WIN, CHAN * CH, 128), BF),
            pltpu.VMEM((CHAN, ROWS_SRC, 128), BF),
            pltpu.VMEM((CHAN, WIN, CH, 128), BF),
            pltpu.VMEM((CHAN, ROWS_SRC, 128), BF),
            pltpu.VMEM((W, 2 * NF), BF),
            pltpu.VMEM((ROWS, 512), BF),
            pltpu.VMEM((ROWS, 2 * NF), F32),
            pltpu.VMEM((ROWS, NF + 256), BF),
            pltpu.SemaphoreType.DMA((CHAN,)),
            pltpu.SemaphoreType.DMA((CHAN,)),
            pltpu.SemaphoreType.DMA((CHAN,)),
            pltpu.SemaphoreType.DMA((CHAN,)),
            pltpu.SemaphoreType.DMA((3,)),
        ],
        compiler_params=pltpu.CompilerParams(
            collective_id=0, has_side_effects=True, vmem_limit_bytes=60 * 1024 * 1024
        ),
        name="spectra",
    )(x, wl, sc.reshape(VS, 1), ca, sa, cb, sb, inverse)


def cross_kernel(a_ref, b_ref, la_ref, ls_ref, cb_ref, sb_ref, out_ref, bi, xk, tt):
    for a in range(8):
        ca = jnp.broadcast_to(la_ref[a:a + 1, :], (64, 128))
        sa = jnp.broadcast_to(ls_ref[a:a + 1, :], (64, 128))
        for kb in range(NKB):
            cols = slice(kb * 128, kb * 128 + 128)
            cols2 = slice(NF + kb * 128, NF + kb * 128 + 128)
            cb, sb = cb_ref[:, cols], sb_ref[:, cols]
            tt[a * 64:a * 64 + 64, cols] = (ca * cb - sa * sb).astype(BF)
            tt[a * 64:a * 64 + 64, cols2] = (-(sa * cb + ca * sb)).astype(BF)

    masks = slot_masks(8)
    diagonal = (
        lax.rem(lax.broadcasted_iota(jnp.int32, (8, 128), 1), 8)
        == lax.broadcasted_iota(jnp.int32, (8, 128), 0)
    )

    def block(kb, _):
        def spread(q, _):
            row = pl.multiple_of(q * 8, 8)
            for ri in range(2):
                col = pl.multiple_of(ri * NF + kb * 128, 128)
                values = []
                for half in range(2):
                    for t in range(3):
                        pair = b_ref[2 * q + half, 16 * t:16 * t + 16, pl.ds(col, 128)].astype(F32)
                        values += [pair[:8], pair[8:]]
                for m, out in enumerate(interleave(values, masks)):
                    bi[m, ri, pl.ds(row, 8), :] = out
            return 0

        lax.fori_loop(0, 16, spread, 0)

        def pair_of_groups(mp, _):
            products = []
            for half in range(2):
                m = 2 * mp + half
                group = kb * 16 + m
                sides = []
                for ri in range(2):
                    tiles = [
                        jnp.where(
                            diagonal,
                            jnp.broadcast_to(a_ref[group, ri, c:c + 1, :], (8, 128)),
                            0.0,
                        )
                        for c in range(CH)
                    ]
                    sides.append(jnp.concatenate(tiles, axis=0).astype(BF))
                left = jnp.concatenate(sides, axis=1)
                bre, bim = bi[m, 0], bi[m, 1]
                right = jnp.concatenate(
                    [
                        jnp.concatenate([bre, bim], axis=1),
                        jnp.concatenate([-bim, bre], axis=1),
                    ],
                    axis=0,
                ).astype(BF)
                products.append(
                    lax.dot_general(
                        left, right, (((1,), (1,)), ((), ())), preferred_element_type=F32
                    )
                )
            row = pl.multiple_of(kb * 128 + mp * 16, 16)
            for ri in range(2):
                for c in range(CH):
                    both = jnp.concatenate(
                        [p[c * 8:c * 8 + 8, ri * 128:ri * 128 + 128] for p in products], axis=0
                    )
                    xk[pl.ds(pl.multiple_of(ri * NF + row, 16), 16), c * 128:c * 128 + 128] = both.astype(BF)
            return 0

        lax.fori_loop(0, 8, pair_of_groups, 0)
        return 0

    lax.fori_loop(0, NKB, block, 0)

    def lags(cb, _):
        col = pl.multiple_of(cb * 256, 256)
        result = jnp.dot(tt[...], xk[:, pl.ds(col, 256)], preferred_element_type=F32)
        for i in range(2):
            flipped = result[:, i * 128:i * 128 + 128].T
            for g in range(SEG):
                out_ref[g, 2 * cb + i] = flipped[32 * g:32 * g + 32].astype(BF)
        return 0

    lax.fori_loop(0, CH // 2, lags, 0)


def cross(a, b, tables):
    _, (cb, sb), (la, ls), _ = tables
    vmem = pl.BlockSpec(memory_space=pltpu.VMEM)
    return pl.pallas_call(
        cross_kernel,
        out_shape=jax.ShapeDtypeStruct((SEG, CH, VS // SEG, LAGS), BF),
        in_specs=[vmem] * 6,
        out_specs=vmem,
        scratch_shapes=[
            pltpu.VMEM((16, 2, VS, 128), F32),
            pltpu.VMEM((2 * NF, CH * VS), BF),
            pltpu.VMEM((LAGS, 2 * NF), BF),
        ],
        compiler_params=pltpu.CompilerParams(vmem_limit_bytes=60 * 1024 * 1024),
        name="cross",
    )(a, b, la, ls, cb, sb)


def on_device(strain_rate, window_length, source_channel):
    tables = small_tables()
    tables = jax.tree.map(jnp.asarray, tables)
    a, b = spectra(strain_rate, window_length, source_channel, tables)
    gathered = lax.all_gather(b, "chan", axis=0, tiled=False)
    shares = cross(a, gathered, tables)
    received = lax.all_to_all(shares, "seg", split_axis=0, concat_axis=0, tiled=True)
    scale = 1.0 / math.sqrt(NF * WIN * SEG)
    return jnp.sum(received.astype(F32), axis=0) * scale


def solution(mesh):
    in_specs = (P("seg", None, "chan"), P("seg"), P())
    out_specs = P("chan", "seg", None)
    return jax.shard_map(
        on_device, mesh=mesh, in_specs=in_specs, out_specs=out_specs, check_vma=False
    )
```

```python
import math

import jax
import jax.numpy as jnp
import numpy as np
from jax import lax
from jax.experimental import pallas as pl
from jax.experimental.pallas import tpu as pltpu
from jax.sharding import PartitionSpec as P

W = 4096
NF = 1152
FIRST_BIN = 16
SMOOTH = 64
MAXLAG = 256
LAGS = 512
VS = 128
CHAN = 32
SEG = 4
WIN = 12
CH = 32
NKB = NF // 128
ROWS_MAIN = WIN * CH
ROWS_SRC = 48
ROWS = ROWS_MAIN + ROWS_SRC
MESH = pl.DeviceIdType.MESH
BF = jnp.bfloat16
F32 = jnp.float32


def unit(product):
    phase = np.mod(product, W).astype(np.float64) * (2.0 * math.pi / W)
    return np.cos(phase).astype(np.float32), np.sin(phase).astype(np.float32)


def small_tables():
    freqs = FIRST_BIN + np.arange(NF)
    coarse = unit(64 * np.arange(64)[:, None] * freqs[None, :128])
    fine = unit(np.arange(64)[:, None] * freqs[None, :])
    lag_coarse = unit(64 * (np.arange(8)[:, None] - 4) * freqs[None, :128])
    width = np.abs(np.arange(NF)[:, None] - np.arange(NF)[None, :]) <= SMOOTH
    inverse = (1.0 / width.sum(axis=0)).astype(np.float32).reshape(1, NF)
    return coarse, fine, lag_coarse, inverse


def slot_masks(rows):
    lane = lax.broadcasted_iota(jnp.int32, (rows, 128), 1)
    return [((lane // 8) // (1 << b)) % 2 == 1 for b in range(4)]


def interleave(values, masks):
    zero = jnp.zeros_like(values[0])
    state = [pltpu.roll(v, 8 * w, 1) if w else v for w, v in enumerate(values)]
    state = state + [zero] * (16 - len(state))
    for b in range(4):
        state = [
            jnp.where(masks[b], state[(i + (1 << b)) % 16], state[i]) for i in range(16)
        ]
    return [state[(-m) % 16] for m in range(16)]


def spectra_kernel(
    x_ref, wl_ref, sc_ref, ca_ref, sa_ref, cb_ref, sb_ref, inv_ref,
    a_out, b_out,
    xv, xs, rm, rs, tab, lhs, acc, magp,
    ssem, rsem, ssem2, rsem2, lsem,
):
    me = lax.axis_index("chan")
    core = lax.rem(me, 2)
    load = pltpu.make_async_copy(x_ref, xv, lsem.at[0])
    load.start()
    barrier = pltpu.get_barrier_semaphore()

    def greet(d, _):
        pl.semaphore_signal(
            barrier, inc=1, device_id={"chan": lax.rem(me + d, CHAN)}, device_id_type=MESH
        )
        return 0

    lax.fori_loop(1, CHAN, greet, 0)
    pl.semaphore_wait(barrier, CHAN - 1)

    def main_copy(d, source):
        peer = lax.rem(me + d, CHAN)
        return pltpu.make_async_remote_copy(
            src_ref=x_ref.at[:, pl.ds(peer * CH, CH), :],
            dst_ref=rm.at[source],
            send_sem=ssem.at[d],
            recv_sem=rsem.at[source],
            device_id={"chan": peer},
            device_id_type=MESH,
        )

    def src_copy(d, source):
        peer = lax.rem(me + d, CHAN)
        return pltpu.make_async_remote_copy(
            src_ref=xs.at[peer],
            dst_ref=rs.at[source],
            send_sem=ssem2.at[d],
            recv_sem=rsem2.at[source],
            device_id={"chan": peer},
            device_id_type=MESH,
        )

    def send(d, _):
        main_copy(d, me).start()
        return 0

    lax.fori_loop(1, CHAN, send, 0)
    own = pltpu.make_async_copy(x_ref.at[:, pl.ds(me * CH, CH), :], rm.at[me], lsem.at[1])
    own.start()

    load.wait()
    hot = (
        lax.broadcasted_iota(jnp.int32, (VS, CHAN * CH), 1) == sc_ref[...]
    ).astype(F32).astype(BF)

    def pick(pair, _):
        first = jnp.dot(hot, xv[2 * pair], preferred_element_type=F32)
        second = jnp.dot(hot, xv[2 * pair + 1], preferred_element_type=F32)
        half = pair // 3
        row = pl.multiple_of(lax.rem(pair, 3) * 16, 16)
        for q in range(16):
            both = jnp.concatenate([first[8 * q:8 * q + 8], second[8 * q:8 * q + 8]], axis=0)
            xs[2 * q + half, pl.ds(row, 16), :] = both.astype(BF)
        return 0

    lax.fori_loop(0, WIN // 2, pick, 0)

    def send_src(d, _):
        src_copy(d, me).start()
        return 0

    lax.fori_loop(1, CHAN, send_src, 0)
    own2 = pltpu.make_async_copy(xs.at[me], rs.at[me], lsem.at[2])
    own2.start()

    def make_rows(a, _):
        row = pl.multiple_of(a * 64, 64)
        ca = jnp.broadcast_to(ca_ref[pl.ds(a, 1), :], (64, 128))
        sa = jnp.broadcast_to(sa_ref[pl.ds(a, 1), :], (64, 128))
        for kb in range(NKB):
            cb = cb_ref[:, kb * 128:kb * 128 + 128]
            sb = sb_ref[:, kb * 128:kb * 128 + 128]
            tab[pl.ds(row, 64), kb * 128:kb * 128 + 128] = (ca * cb - sa * sb).astype(BF)
            tab[pl.ds(row, 64), NF + kb * 128:NF + kb * 128 + 128] = (
                -(sa * cb + ca * sb)
            ).astype(BF)
        return 0

    lax.fori_loop(0, 64, make_rows, 0)
    acc[...] = jnp.zeros_like(acc)
    own.wait()
    own2.wait()

    lane = lax.broadcasted_iota(jnp.int32, (1, 128), 1)

    def gather_group(step, _):
        group = lax.rem(me // 4 + CHAN // 4 - step, CHAN // 4)
        for i in range(4):
            j = group * 4 + i

            @pl.when(j != me)
            def _():
                main_copy(0, j).wait_recv()
                src_copy(0, j).wait_recv()

            def keep(w):
                inside = lane + j * 128 < wl_ref[w]
                return jnp.where(inside, 1.0, 0.0).astype(BF)

            for w in range(WIN):
                lhs[w * CH:(w + 1) * CH, i * 128:(i + 1) * 128] = rm[j, w] * keep(w)
            for t in range(3):
                upper = jnp.broadcast_to(keep(core * 6 + 2 * t).astype(F32), (8, 128))
                lower = jnp.broadcast_to(keep(core * 6 + 2 * t + 1).astype(F32), (8, 128))
                both = jnp.concatenate([upper, lower], axis=0).astype(BF)
                lhs[ROWS_MAIN + 16 * t:ROWS_MAIN + 16 * t + 16, i * 128:(i + 1) * 128] = (
                    rs[j, 16 * t:16 * t + 16, :] * both
                )

        def column(ct, _):
            col = pl.multiple_of(ct * 256, 256)
            row = pl.multiple_of(group * 512, 512)
            acc[:, pl.ds(col, 256)] += jnp.dot(
                lhs[...], tab[pl.ds(row, 512), pl.ds(col, 256)], preferred_element_type=F32
            )
            return 0

        lax.fori_loop(0, 2 * NF // 256, column, 0)
        return 0

    lax.fori_loop(0, CHAN // 4, gather_group, 0)

    def sent(d, _):
        main_copy(d, me).wait_send()
        src_copy(d, me).wait_send()
        return 0

    lax.fori_loop(1, CHAN, sent, 0)

    magp[:, 0:128] = jnp.zeros((ROWS, 128), BF)
    magp[:, NF + 128:NF + 256] = jnp.zeros((ROWS, 128), BF)

    def magnitude(kb, _):
        col = pl.multiple_of(kb * 128, 128)
        re = acc[:, pl.ds(col, 128)]
        im = acc[:, pl.ds(pl.multiple_of(NF + col, 128), 128)]
        magp[:, pl.ds(pl.multiple_of(col + 128, 128), 128)] = jnp.sqrt(re * re + im * im).astype(BF)
        return 0

    lax.fori_loop(0, NKB, magnitude, 0)
    band = (
        jnp.abs(
            lax.broadcasted_iota(jnp.int32, (384, 128), 0)
            - 128
            - lax.broadcasted_iota(jnp.int32, (384, 128), 1)
        )
        <= SMOOTH
    ).astype(F32).astype(BF)

    def whiten(kb, _):
        col = pl.multiple_of(kb * 128, 128)
        col2 = pl.multiple_of(NF + col, 128)
        total = jnp.dot(magp[:, pl.ds(col, 384)], band, preferred_element_type=F32)
        scale = 1.0 / (total * inv_ref[:, pl.ds(col, 128)] + 1e-06)
        acc[:, pl.ds(col, 128)] = acc[:, pl.ds(col, 128)] * scale
        acc[:, pl.ds(col2, 128)] = acc[:, pl.ds(col2, 128)] * scale
        return 0

    lax.fori_loop(0, NKB, whiten, 0)

    b_out[...] = acc[ROWS_MAIN:, :].astype(BF)
    masks = slot_masks(8)

    def spread(step, _):
        kb = step // 4
        c8 = pl.multiple_of(lax.rem(step, 4) * 8, 8)
        for ri in range(2):
            col = pl.multiple_of(ri * NF + kb * 128, 128)
            values = [
                acc[pl.ds(pl.multiple_of(w * CH + c8, 8), 8), pl.ds(col, 128)] for w in range(WIN)
            ]
            for m, out in enumerate(interleave(values, masks)):
                a_out[kb * 16 + m, ri, pl.ds(c8, 8), :] = out
        return 0

    lax.fori_loop(0, NKB * 4, spread, 0)


def spectra(x, wl, sc, tables):
    (ca, sa), (cb, sb), _, inverse = tables
    vmem = pl.BlockSpec(memory_space=pltpu.VMEM)
    return pl.pallas_call(
        spectra_kernel,
        out_shape=(
            jax.ShapeDtypeStruct((NKB * 16, 2, CH, 128), F32),
            jax.ShapeDtypeStruct((ROWS_SRC, 2 * NF), BF),
        ),
        in_specs=[
            pl.BlockSpec(memory_space=pl.ANY),
            pl.BlockSpec(memory_space=pltpu.SMEM),
            vmem, vmem, vmem, vmem, vmem, vmem,
        ],
        out_specs=(vmem, vmem),
        scratch_shapes=[
            pltpu.VMEM((WIN, CHAN * CH, 128), BF),
            pltpu.VMEM((CHAN, ROWS_SRC, 128), BF),
            pltpu.VMEM((CHAN, WIN, CH, 128), BF),
            pltpu.VMEM((CHAN, ROWS_SRC, 128), BF),
            pltpu.VMEM((W, 2 * NF), BF),
            pltpu.VMEM((ROWS, 512), BF),
            pltpu.VMEM((ROWS, 2 * NF), F32),
            pltpu.VMEM((ROWS, NF + 256), BF),
            pltpu.SemaphoreType.DMA((CHAN,)),
            pltpu.SemaphoreType.DMA((CHAN,)),
            pltpu.SemaphoreType.DMA((CHAN,)),
            pltpu.SemaphoreType.DMA((CHAN,)),
            pltpu.SemaphoreType.DMA((3,)),
        ],
        compiler_params=pltpu.CompilerParams(
            collective_id=0, has_side_effects=True, vmem_limit_bytes=60 * 1024 * 1024
        ),
        name="spectra",
    )(x, wl, sc.reshape(VS, 1), ca, sa, cb, sb, inverse)


NC = 3
CKB = NKB // NC
CL = CKB * 128


def cross_kernel(
    a_hbm, b_hbm, la_ref, ls_ref, cb_ref, sb_ref, out_ref,
    a_ref, g_ref, bi, xk, tt, mine, share, landed,
    s1, r1, s2, r2, s3, r3, s4, r4, sx, rx, lsem,
):
    me = lax.axis_index("chan")
    seg = lax.axis_index("seg")
    z, y, core = me // 8, lax.rem(me // 2, 4), lax.rem(me, 2)
    load = pltpu.make_async_copy(a_hbm, a_ref, lsem.at[0])
    load.start()

    def at(zz, yy, cc):
        return {"chan": lax.rem(zz + 4, 4) * 8 + lax.rem(yy + 4, 4) * 2 + cc}

    def beyond(axis, d):
        return at(z + d, y, core) if axis == 0 else at(z, y + d, core)

    def segment(d):
        return {"seg": lax.rem(seg + d, SEG)}

    barrier = pltpu.get_barrier_semaphore()
    for d in (1, 2, 3):
        for who in (beyond(0, d), beyond(1, d), segment(d)):
            pl.semaphore_signal(barrier, inc=1, device_id=who, device_id_type=MESH)
    pl.semaphore_signal(barrier, inc=1, device_id=at(z, y, 1 - core), device_id_type=MESH)
    pl.semaphore_wait(barrier, 10)

    def remote(src, dst, send, recv, who):
        return pltpu.make_async_remote_copy(
            src_ref=src, dst_ref=dst, send_sem=send, recv_sem=recv, device_id=who, device_id_type=MESH
        )

    def block(ch, ri):
        return b_hbm.at[:, ri * NF + ch * CL:ri * NF + (ch + 1) * CL]

    def first(ch, ri, d):
        k = (ch * 2 + ri) * 3 + d - 1
        return remote(block(ch, ri), g_ref.at[ch, ri, core, z, y], s1.at[k], r1.at[k], beyond(ri, d))

    def line(ch, ri, start, size, d):
        if ri == 0:
            return g_ref.at[ch, ri, core, start:start + size, lax.rem(y + d + 4, 4)]
        return g_ref.at[ch, ri, core, lax.rem(z + d + 4, 4), start:start + size]

    def second(ch, ri, way):
        k = (ch * 2 + ri) * 2 + way
        d = 1 if way == 0 else 3
        whole = line(ch, ri, 0, 4, 0)
        return remote(whole, whole, s2.at[k], r2.at[k], beyond(1 - ri, d))

    def third(ch, ri, way):
        k = (ch * 2 + ri) * 2 + way
        d = 1 if way == 0 else 3
        part = line(ch, ri, 2 * way, 2, -1 if way == 0 else 1)
        return remote(part, part, s3.at[k], r3.at[k], beyond(1 - ri, d))

    def fourth(ch, ri):
        k = ch * 2 + ri
        part = g_ref.at[ch, ri, core]
        return remote(part, part, s4.at[k], r4.at[k], at(z, y, 1 - core))

    def own(ch, ri):
        return pltpu.make_async_copy(block(ch, ri), g_ref.at[ch, ri, core, z, y], lsem.at[1 + ch * 2 + ri])

    halves = (0, 1)
    for ch in range(NC):
        for ri in halves:
            for d in (2, 1, 3):
                first(ch, ri, d).start()
            own(ch, ri).start()

    for a in range(8):
        ca = jnp.broadcast_to(la_ref[a:a + 1, :], (64, 128))
        sa = jnp.broadcast_to(ls_ref[a:a + 1, :], (64, 128))
        for kb in range(NKB):
            cols = slice(kb * 128, kb * 128 + 128)
            cols2 = slice(NF + kb * 128, NF + kb * 128 + 128)
            cb, sb = cb_ref[:, cols], sb_ref[:, cols]
            tt[a * 64:a * 64 + 64, cols] = (ca * cb - sa * sb).astype(BF)
            tt[a * 64:a * 64 + 64, cols2] = (-(sa * cb + ca * sb)).astype(BF)

    masks = slot_masks(8)
    diagonal = (
        lax.rem(lax.broadcasted_iota(jnp.int32, (8, 128), 1), 8)
        == lax.broadcasted_iota(jnp.int32, (8, 128), 0)
    )

    def step_second(ch):
        for ri in halves:
            for d in (1, 2, 3):
                first(ch, ri, d).wait_recv()
            own(ch, ri).wait()
            for way in (0, 1):
                second(ch, ri, way).start()

    def step_third(ch):
        for ri in halves:
            for way in (0, 1):
                second(ch, ri, way).wait_recv()
                third(ch, ri, way).start()

    def step_fourth(ch):
        for ri in halves:
            for way in (0, 1):
                third(ch, ri, way).wait_recv()
            fourth(ch, ri).start()

    def arrived(ch):
        for ri in halves:
            fourth(ch, ri).wait_recv()

    def bins(ch, kbl):
        kb = ch * CKB + kbl

        def spread(q, _):
            row = pl.multiple_of(q * 8, 8)
            for ri in range(2):
                col = kbl * 128
                values = []
                for half in range(2):
                    for t in range(3):
                        pair = g_ref[
                            ch, ri, half, q // 4, lax.rem(q, 4), 16 * t:16 * t + 16, col:col + 128
                        ].astype(F32)
                        values += [pair[:8], pair[8:]]
                for m, out in enumerate(interleave(values, masks)):
                    bi[m, ri, pl.ds(row, 8), :] = out
            return 0

        lax.fori_loop(0, 16, spread, 0)

        def pair_of_groups(mp, _):
            products = []
            for half in range(2):
                m = 2 * mp + half
                group = kb * 16 + m
                sides = []
                for ri in range(2):
                    tiles = [
                        jnp.where(
                            diagonal,
                            jnp.broadcast_to(a_ref[group, ri, c:c + 1, :], (8, 128)),
                            0.0,
                        )
                        for c in range(CH)
                    ]
                    sides.append(jnp.concatenate(tiles, axis=0).astype(BF))
                left = jnp.concatenate(sides, axis=1)
                bre, bim = bi[m, 0], bi[m, 1]
                right = jnp.concatenate(
                    [
                        jnp.concatenate([bre, bim], axis=1),
                        jnp.concatenate([-bim, bre], axis=1),
                    ],
                    axis=0,
                ).astype(BF)
                products.append(
                    lax.dot_general(
                        left, right, (((1,), (1,)), ((), ())), preferred_element_type=F32
                    )
                )
            row = pl.multiple_of(kb * 128 + mp * 16, 16)
            for ri in range(2):
                for c in range(CH):
                    both = jnp.concatenate(
                        [p[c * 8:c * 8 + 8, ri * 128:ri * 128 + 128] for p in products], axis=0
                    )
                    xk[pl.ds(pl.multiple_of(ri * NF + row, 16), 16), c * 128:c * 128 + 128] = both.astype(BF)
            return 0

        lax.fori_loop(0, 8, pair_of_groups, 0)

    for ch in range(NC):
        step_second(ch)
    step_third(0)
    step_third(1)
    step_fourth(0)
    load.wait()
    arrived(0)
    bins(0, 0)
    step_third(2)
    step_fourth(1)
    bins(0, 1)
    step_fourth(2)
    bins(0, 2)
    for ch in range(1, NC):
        arrived(ch)
        for kbl in range(CKB):
            bins(ch, kbl)

    def exchange(block4, d):
        c0 = pl.multiple_of(block4 * 4, 4)
        return remote(
            share.at[lax.rem(seg + d, SEG), pl.ds(c0, 4)],
            landed.at[d - 1, pl.ds(c0, 4)],
            sx.at[d - 1, block4],
            rx.at[d - 1, block4],
            segment(d),
        )

    def lags(block4, _):
        for i2 in range(2):
            cb = block4 * 2 + i2
            col = pl.multiple_of(cb * 256, 256)
            result = jnp.dot(tt[...], xk[:, pl.ds(col, 256)], preferred_element_type=F32)
            for i in range(2):
                flipped = result[:, i * 128:i * 128 + 128].T
                for g in range(SEG):
                    part = flipped[32 * g:32 * g + 32]
                    share[g, 2 * cb + i] = part.astype(BF)

                    @pl.when(seg == g)
                    def _():
                        mine[2 * cb + i] = part

        for d in (2, 1, 3):
            exchange(block4, d).start()
        return 0

    lax.fori_loop(0, CH // 4, lags, 0)

    scale = 1.0 / math.sqrt(NF * WIN * SEG)

    def finish(block4, _):
        for d in (1, 2, 3):
            exchange(block4, d).wait_recv()
        c0 = pl.multiple_of(block4 * 4, 4)
        total = mine[pl.ds(c0, 4)]
        for d in (1, 2, 3):
            total = total + landed[d - 1, pl.ds(c0, 4)].astype(F32)
        out_ref[pl.ds(c0, 4)] = total * scale
        return 0

    lax.fori_loop(0, CH // 4, finish, 0)

    for ch in range(NC):
        for ri in halves:
            for d in (1, 2, 3):
                first(ch, ri, d).wait_send()
            for way in (0, 1):
                second(ch, ri, way).wait_send()
                third(ch, ri, way).wait_send()
            fourth(ch, ri).wait_send()

    def sent(block4, _):
        for d in (1, 2, 3):
            exchange(block4, d).wait_send()
        return 0

    lax.fori_loop(0, CH // 4, sent, 0)


def cross(a, b, tables):
    _, (cb, sb), (la, ls), _ = tables
    vmem = pl.BlockSpec(memory_space=pltpu.VMEM)
    hbm = pl.BlockSpec(memory_space=pl.ANY)
    dma = pltpu.SemaphoreType.DMA
    return pl.pallas_call(
        cross_kernel,
        out_shape=jax.ShapeDtypeStruct((CH, VS // SEG, LAGS), F32),
        in_specs=[hbm, hbm] + [vmem] * 4,
        out_specs=vmem,
        scratch_shapes=[
            pltpu.VMEM((NKB * 16, 2, CH, 128), F32),
            pltpu.VMEM((NC, 2, 2, 4, 4, ROWS_SRC, CL), BF),
            pltpu.VMEM((16, 2, VS, 128), F32),
            pltpu.VMEM((2 * NF, CH * VS), BF),
            pltpu.VMEM((LAGS, 2 * NF), BF),
            pltpu.VMEM((CH, VS // SEG, LAGS), F32),
            pltpu.VMEM((SEG, CH, VS // SEG, LAGS), BF),
            pltpu.VMEM((SEG - 1, CH, VS // SEG, LAGS), BF),
            dma((NC * 6,)), dma((NC * 6,)),
            dma((NC * 4,)), dma((NC * 4,)),
            dma((NC * 4,)), dma((NC * 4,)),
            dma((NC * 2,)), dma((NC * 2,)),
            dma((SEG - 1, CH // 4)), dma((SEG - 1, CH // 4)),
            dma((1 + NC * 2,)),
        ],
        compiler_params=pltpu.CompilerParams(
            collective_id=1, has_side_effects=True, vmem_limit_bytes=60 * 1024 * 1024
        ),
        name="cross",
    )(a, b, la, ls, cb, sb)


def on_device(strain_rate, window_length, source_channel):
    tables = jax.tree.map(jnp.asarray, small_tables())
    a, b = spectra(strain_rate, window_length, source_channel, tables)
    return cross(a, b, tables)


def solution(mesh):
    in_specs = (P("seg", None, "chan"), P("seg"), P())
    out_specs = P("chan", "seg", None)
    return jax.shard_map(
        on_device, mesh=mesh, in_specs=in_specs, out_specs=out_specs, check_vma=False
    )
```

```python
import math

import jax
import jax.numpy as jnp
import numpy as np
from jax import lax
from jax.experimental import pallas as pl
from jax.experimental.pallas import tpu as pltpu
from jax.sharding import PartitionSpec as P

W = 4096
NF = 1152
FIRST_BIN = 16
SMOOTH = 64
MAXLAG = 256
LAGS = 512
VS = 128
CHAN = 32
SEG = 4
WIN = 12
CH = 32
NKB = NF // 128
ROWS_MAIN = WIN * CH
ROWS_SRC = 48
ROWS = ROWS_MAIN + ROWS_SRC
GROUPS = (8, 8, 8, 4, 4)
MESH = pl.DeviceIdType.MESH
BF = jnp.bfloat16
F32 = jnp.float32


def unit(product):
    phase = np.mod(product, W).astype(np.float64) * (2.0 * math.pi / W)
    return np.cos(phase).astype(np.float32), np.sin(phase).astype(np.float32)


def small_tables():
    freqs = FIRST_BIN + np.arange(NF)
    coarse = unit(64 * np.arange(64)[:, None] * freqs[None, :128])
    fine = unit(np.arange(64)[:, None] * freqs[None, :])
    lag_coarse = unit(64 * (np.arange(8)[:, None] - 4) * freqs[None, :128])
    width = np.abs(np.arange(NF)[:, None] - np.arange(NF)[None, :]) <= SMOOTH
    inverse = (1.0 / width.sum(axis=0)).astype(np.float32).reshape(1, NF)
    return coarse, fine, lag_coarse, inverse


def slot_masks(rows):
    lane = lax.broadcasted_iota(jnp.int32, (rows, 128), 1)
    return [((lane // 8) // (1 << b)) % 2 == 1 for b in range(4)]


def interleave(values, masks):
    zero = jnp.zeros_like(values[0])
    state = [pltpu.roll(v, 8 * w, 1) if w else v for w, v in enumerate(values)]
    state = state + [zero] * (16 - len(state))
    for b in range(4):
        state = [
            jnp.where(masks[b], state[(i + (1 << b)) % 16], state[i]) for i in range(16)
        ]
    return [state[(-m) % 16] for m in range(16)]


def spectra_kernel(
    x_ref, wl_ref, sc_ref, ca_ref, sa_ref, cb_ref, sb_ref, inv_ref,
    a_out, b_out,
    xv, xs, rm, rs, tab, lhs, acc, magp,
    ssem, rsem, ssem2, rsem2, lsem,
):
    me = lax.axis_index("chan")
    core = lax.rem(me, 2)
    load = pltpu.make_async_copy(x_ref, xv, lsem.at[0])
    load.start()
    barrier = pltpu.get_barrier_semaphore()

    def greet(d, _):
        pl.semaphore_signal(
            barrier, inc=1, device_id={"chan": lax.rem(me + d, CHAN)}, device_id_type=MESH
        )
        return 0

    lax.fori_loop(1, CHAN, greet, 0)
    pl.semaphore_wait(barrier, CHAN - 1)

    def sender(d):
        return lax.rem(me + CHAN * 13 - 13 * d, CHAN)

    def main_copy(d):
        peer = lax.rem(me + 13 * d, CHAN)
        return pltpu.make_async_remote_copy(
            src_ref=x_ref.at[:, pl.ds(peer * CH, CH), :],
            dst_ref=rm.at[d],
            send_sem=ssem.at[d],
            recv_sem=rsem.at[d],
            device_id={"chan": peer},
            device_id_type=MESH,
        )

    def src_copy(d):
        peer = lax.rem(me + 13 * d, CHAN)
        return pltpu.make_async_remote_copy(
            src_ref=xs.at[peer],
            dst_ref=rs.at[d],
            send_sem=ssem2.at[d],
            recv_sem=rsem2.at[d],
            device_id={"chan": peer},
            device_id_type=MESH,
        )

    def send(d, _):
        main_copy(d).start()
        return 0

    lax.fori_loop(1, 8, send, 0)
    own = pltpu.make_async_copy(x_ref.at[:, pl.ds(me * CH, CH), :], rm.at[0], lsem.at[1])
    own.start()

    load.wait()
    hot = (
        lax.broadcasted_iota(jnp.int32, (VS, CHAN * CH), 1) == sc_ref[...]
    ).astype(F32).astype(BF)

    def pick(pair, _):
        first = jnp.dot(hot, xv[2 * pair], preferred_element_type=F32)
        second = jnp.dot(hot, xv[2 * pair + 1], preferred_element_type=F32)
        half = pair // 3
        row = pl.multiple_of(lax.rem(pair, 3) * 16, 16)
        for q in range(16):
            both = jnp.concatenate([first[8 * q:8 * q + 8], second[8 * q:8 * q + 8]], axis=0)
            xs[2 * q + half, pl.ds(row, 16), :] = both.astype(BF)
        return 0

    lax.fori_loop(0, WIN // 2, pick, 0)

    def send_src(d, _):
        src_copy(d).start()
        return 0

    lax.fori_loop(1, CHAN, send_src, 0)
    lax.fori_loop(8, CHAN, send, 0)
    own2 = pltpu.make_async_copy(xs.at[me], rs.at[0], lsem.at[2])
    own2.start()

    def make_rows(a, _):
        row = pl.multiple_of(a * 64, 64)
        ca = jnp.broadcast_to(ca_ref[pl.ds(a, 1), :], (64, 128))
        sa = jnp.broadcast_to(sa_ref[pl.ds(a, 1), :], (64, 128))
        for kb in range(NKB):
            cb = cb_ref[:, kb * 128:kb * 128 + 128]
            sb = sb_ref[:, kb * 128:kb * 128 + 128]
            tab[pl.ds(row, 64), kb * 128:kb * 128 + 128] = (ca * cb - sa * sb).astype(BF)
            tab[pl.ds(row, 64), NF + kb * 128:NF + kb * 128 + 128] = (
                -(sa * cb + ca * sb)
            ).astype(BF)
        return 0

    lax.fori_loop(0, 64, make_rows, 0)

    lane = lax.broadcasted_iota(jnp.int32, (1, 128), 1)

    def arrive(d, _):
        main_copy(d).wait_recv()
        src_copy(d).wait_recv()
        return 0

    begin = 0
    for size in GROUPS:
        if begin == 0:
            own.wait()
            own2.wait()
        lax.fori_loop(max(begin, 1), begin + size, arrive, 0)
        for i in range(size):
            d = begin + i
            j = sender(d)

            def keep(w):
                inside = lane + j * 128 < wl_ref[w]
                return jnp.where(inside, 1.0, 0.0)

            for w in range(WIN):
                lhs[w * CH:(w + 1) * CH, i * 128:(i + 1) * 128] = rm[d, w] * keep(w).astype(BF)
            for t in range(3):
                upper = jnp.broadcast_to(keep(core * 6 + 2 * t), (8, 128))
                lower = jnp.broadcast_to(keep(core * 6 + 2 * t + 1), (8, 128))
                both = jnp.concatenate([upper, lower], axis=0).astype(BF)
                lhs[ROWS_MAIN + 16 * t:ROWS_MAIN + 16 * t + 16, i * 128:(i + 1) * 128] = (
                    rs[d, 16 * t:16 * t + 16, :] * both
                )

        def column(ct, _, begin=begin, size=size):
            col = pl.multiple_of(ct * 256, 256)
            right = jnp.concatenate(
                [
                    tab[pl.ds(pl.multiple_of(sender(begin + i) * 128, 128), 128), pl.ds(col, 256)]
                    for i in range(size)
                ],
                axis=0,
            )
            part = jnp.dot(lhs[:, :size * 128], right, preferred_element_type=F32)
            if begin:
                part = part + acc[:, pl.ds(col, 256)]
            acc[:, pl.ds(col, 256)] = part
            return 0

        lax.fori_loop(0, 2 * NF // 256, column, 0)
        begin += size

    def sent(d, _):
        main_copy(d).wait_send()
        src_copy(d).wait_send()
        return 0

    lax.fori_loop(1, CHAN, sent, 0)

    magp[:, 0:128] = jnp.zeros((ROWS, 128), BF)
    magp[:, NF + 128:NF + 256] = jnp.zeros((ROWS, 128), BF)

    def magnitude(kb, _):
        col = pl.multiple_of(kb * 128, 128)
        re = acc[:, pl.ds(col, 128)]
        im = acc[:, pl.ds(pl.multiple_of(NF + col, 128), 128)]
        magp[:, pl.ds(pl.multiple_of(col + 128, 128), 128)] = jnp.sqrt(re * re + im * im).astype(BF)
        return 0

    lax.fori_loop(0, NKB, magnitude, 0)
    band = (
        jnp.abs(
            lax.broadcasted_iota(jnp.int32, (384, 128), 0)
            - 128
            - lax.broadcasted_iota(jnp.int32, (384, 128), 1)
        )
        <= SMOOTH
    ).astype(F32).astype(BF)

    def whiten(kb, _):
        col = pl.multiple_of(kb * 128, 128)
        col2 = pl.multiple_of(NF + col, 128)
        total = jnp.dot(magp[:, pl.ds(col, 384)], band, preferred_element_type=F32)
        scale = 1.0 / (total * inv_ref[:, pl.ds(col, 128)] + 1e-06)
        acc[:, pl.ds(col, 128)] = acc[:, pl.ds(col, 128)] * scale
        acc[:, pl.ds(col2, 128)] = acc[:, pl.ds(col2, 128)] * scale
        return 0

    lax.fori_loop(0, NKB, whiten, 0)

    b_out[...] = acc[ROWS_MAIN:, :].astype(BF)
    masks = slot_masks(8)

    def spread(step, _):
        kb = step // 2
        for part in range(2):
            c8 = pl.multiple_of(lax.rem(step, 2) * 16 + part * 8, 8)
            for ri in range(2):
                col = pl.multiple_of(ri * NF + kb * 128, 128)
                values = [
                    acc[pl.ds(pl.multiple_of(w * CH + c8, 8), 8), pl.ds(col, 128)] for w in range(WIN)
                ]
                for m, out in enumerate(interleave(values, masks)):
                    a_out[kb * 16 + m, ri, lax.rem(step, 2) * 2 + part] = out
        return 0

    lax.fori_loop(0, NKB * 2, spread, 0)


def spectra(x, wl, sc, tables):
    (ca, sa), (cb, sb), _, inverse = tables
    vmem = pl.BlockSpec(memory_space=pltpu.VMEM)
    return pl.pallas_call(
        spectra_kernel,
        out_shape=(
            jax.ShapeDtypeStruct((NKB * 16, 2, CH // 8, 8, 128), F32),
            jax.ShapeDtypeStruct((ROWS_SRC, 2 * NF), BF),
        ),
        in_specs=[
            pl.BlockSpec(memory_space=pl.ANY),
            pl.BlockSpec(memory_space=pltpu.SMEM),
            vmem, vmem, vmem, vmem, vmem, vmem,
        ],
        out_specs=(vmem, vmem),
        scratch_shapes=[
            pltpu.VMEM((WIN, CHAN * CH, 128), BF),
            pltpu.VMEM((CHAN, ROWS_SRC, 128), BF),
            pltpu.VMEM((CHAN, WIN, CH, 128), BF),
            pltpu.VMEM((CHAN, ROWS_SRC, 128), BF),
            pltpu.VMEM((W, 2 * NF), BF),
            pltpu.VMEM((ROWS, 1024), BF),
            pltpu.VMEM((ROWS, 2 * NF), F32),
            pltpu.VMEM((ROWS, NF + 256), BF),
            pltpu.SemaphoreType.DMA((CHAN,)),
            pltpu.SemaphoreType.DMA((CHAN,)),
            pltpu.SemaphoreType.DMA((CHAN,)),
            pltpu.SemaphoreType.DMA((CHAN,)),
            pltpu.SemaphoreType.DMA((3,)),
        ],
        compiler_params=pltpu.CompilerParams(
            collective_id=0, has_side_effects=True, vmem_limit_bytes=60 * 1024 * 1024
        ),
        name="spectra",
    )(x, wl, sc.reshape(VS, 1), ca, sa, cb, sb, inverse)


NC = 3
CKB = NKB // NC
CL = CKB * 128
NQ = 4
CQ = CH // NQ


def cross_kernel(
    a_hbm, b_hbm, la_ref, ls_ref, cb_ref, sb_ref, out_ref,
    a_ref, g_ref, bi, xk, tt, mine, share, landed,
    s1, r1, s2, r2, s3, r3, s4, r4, sx, rx, lsem,
):
    me = lax.axis_index("chan")
    seg = lax.axis_index("seg")
    z, y, core = me // 8, lax.rem(me // 2, 4), lax.rem(me, 2)
    load = pltpu.make_async_copy(a_hbm, a_ref, lsem.at[0])
    load.start()

    def at(zz, yy, cc):
        return {"chan": lax.rem(zz + 4, 4) * 8 + lax.rem(yy + 4, 4) * 2 + cc}

    def beyond(axis, d):
        return at(z + d, y, core) if axis == 0 else at(z, y + d, core)

    def segment(d):
        return {"seg": lax.rem(seg + d, SEG)}

    barrier = pltpu.get_barrier_semaphore()
    for d in (1, 2, 3):
        for who in (beyond(0, d), beyond(1, d), segment(d)):
            pl.semaphore_signal(barrier, inc=1, device_id=who, device_id_type=MESH)
    pl.semaphore_signal(barrier, inc=1, device_id=at(z, y, 1 - core), device_id_type=MESH)
    pl.semaphore_wait(barrier, 10)

    def remote(src, dst, send, recv, who):
        return pltpu.make_async_remote_copy(
            src_ref=src, dst_ref=dst, send_sem=send, recv_sem=recv, device_id=who, device_id_type=MESH
        )

    def block(ch, ri):
        return b_hbm.at[:, ri * NF + ch * CL:ri * NF + (ch + 1) * CL]

    def first(ch, ri, d):
        k = (ch * 2 + ri) * 3 + d - 1
        return remote(block(ch, ri), g_ref.at[ch, ri, core, z, y], s1.at[k], r1.at[k], beyond(ri, d))

    def line(ch, ri, start, size, d):
        if ri == 0:
            return g_ref.at[ch, ri, core, start:start + size, lax.rem(y + d + 4, 4)]
        return g_ref.at[ch, ri, core, lax.rem(z + d + 4, 4), start:start + size]

    def second(ch, ri, way):
        k = (ch * 2 + ri) * 2 + way
        d = 1 if way == 0 else 3
        whole = line(ch, ri, 0, 4, 0)
        return remote(whole, whole, s2.at[k], r2.at[k], beyond(1 - ri, d))

    def third(ch, ri, way):
        k = (ch * 2 + ri) * 2 + way
        d = 1 if way == 0 else 3
        part = line(ch, ri, 2 * way, 2, -1 if way == 0 else 1)
        return remote(part, part, s3.at[k], r3.at[k], beyond(1 - ri, d))

    def fourth(ch, ri):
        k = ch * 2 + ri
        part = g_ref.at[ch, ri, core]
        return remote(part, part, s4.at[k], r4.at[k], at(z, y, 1 - core))

    def own(ch, ri):
        return pltpu.make_async_copy(block(ch, ri), g_ref.at[ch, ri, core, z, y], lsem.at[1 + ch * 2 + ri])

    halves = (0, 1)
    for ch in range(NC):
        for ri in halves:
            for d in (2, 1, 3):
                first(ch, ri, d).start()
            own(ch, ri).start()

    for a in range(8):
        ca = jnp.broadcast_to(la_ref[a:a + 1, :], (64, 128))
        sa = jnp.broadcast_to(ls_ref[a:a + 1, :], (64, 128))
        for kb in range(NKB):
            cols = slice(kb * 128, kb * 128 + 128)
            cols2 = slice(NF + kb * 128, NF + kb * 128 + 128)
            cb, sb = cb_ref[:, cols], sb_ref[:, cols]
            tt[a * 64:a * 64 + 64, cols] = (ca * cb - sa * sb).astype(BF)
            tt[a * 64:a * 64 + 64, cols2] = (-(sa * cb + ca * sb)).astype(BF)

    masks = slot_masks(8)
    diagonal = (
        lax.rem(lax.broadcasted_iota(jnp.int32, (8, 128), 1), 8)
        == lax.broadcasted_iota(jnp.int32, (8, 128), 0)
    )

    def step_second(ch):
        for ri in halves:
            for d in (1, 2, 3):
                first(ch, ri, d).wait_recv()
            own(ch, ri).wait()
            for way in (0, 1):
                second(ch, ri, way).start()

    def step_third(ch):
        for ri in halves:
            for way in (0, 1):
                second(ch, ri, way).wait_recv()
                third(ch, ri, way).start()

    def step_fourth(ch):
        for ri in halves:
            for way in (0, 1):
                third(ch, ri, way).wait_recv()
            fourth(ch, ri).start()

    def arrived(ch):
        for ri in halves:
            fourth(ch, ri).wait_recv()

    def bins(ch, kbl):
        kb = ch * CKB + kbl

        def spread(qq, _):
            row = pl.multiple_of(qq * 16, 16)
            for ri in range(2):
                col = kbl * 128
                outs = []
                for q2 in range(2):
                    q = 2 * qq + q2
                    values = []
                    for half in range(2):
                        for t in range(3):
                            pair = g_ref[
                                ch, ri, half, q // 4, lax.rem(q, 4), 16 * t:16 * t + 16, col:col + 128
                            ].astype(F32)
                            values += [pair[:8], pair[8:]]
                    outs.append(interleave(values, masks))
                for m in range(16):
                    both = jnp.concatenate([outs[0][m], outs[1][m]], axis=0)
                    bi[kb * 16 + m, pl.ds(row, 16), ri * 128:ri * 128 + 128] = both.astype(BF)
            return 0

        lax.fori_loop(0, 8, spread, 0)

    def products(cq):
        def several(it, _):
            for p in range(NQ):
                mp = it * NQ + p
                results = []
                for half in range(2):
                    group = 2 * mp + half
                    sides = []
                    for ri in range(2):
                        tiles = [
                            jnp.where(
                                diagonal,
                                jnp.broadcast_to(
                                    a_ref[group, ri, cq * (CQ // 8) + c // 8, c % 8:c % 8 + 1, :], (8, 128)
                                ),
                                0.0,
                            )
                            for c in range(CQ)
                        ]
                        sides.append(jnp.concatenate(tiles, axis=0).astype(BF))
                    left = jnp.concatenate(sides, axis=1)
                    bre = bi[group, :, 0:128]
                    bim = bi[group, :, 128:256]
                    right = jnp.concatenate(
                        [
                            jnp.concatenate([bre, bim], axis=1),
                            jnp.concatenate([-bim, bre], axis=1),
                        ],
                        axis=0,
                    )
                    results.append(
                        lax.dot_general(
                            left, right, (((1,), (1,)), ((), ())), preferred_element_type=F32
                        )
                    )
                row = pl.multiple_of(mp * 16, 16)
                for ri in range(2):
                    for c in range(CQ):
                        both = jnp.concatenate(
                            [r[c * 8:c * 8 + 8, ri * 128:ri * 128 + 128] for r in results], axis=0
                        )
                        xk[pl.ds(pl.multiple_of(ri * NF + row, 16), 16), c * 128:c * 128 + 128] = both.astype(BF)
            return 0

        lax.fori_loop(0, NKB * 8 // NQ, several, 0)

    for ch in range(NC):
        step_second(ch)
    step_third(0)
    step_third(1)
    step_fourth(0)
    load.wait()
    arrived(0)
    bins(0, 0)
    step_third(2)
    step_fourth(1)
    bins(0, 1)
    step_fourth(2)
    bins(0, 2)
    for ch in range(1, NC):
        arrived(ch)
        for kbl in range(CKB):
            bins(ch, kbl)

    def exchange(part, d):
        c0 = pl.multiple_of(part * CQ, CQ)
        return remote(
            share.at[lax.rem(seg + d, SEG), pl.ds(c0, CQ)],
            landed.at[d - 1, pl.ds(c0, CQ)],
            sx.at[d - 1, part],
            rx.at[d - 1, part],
            segment(d),
        )

    def quarter(cq, _):
        products(cq)

        def lags(cb, _):
            col = pl.multiple_of(cb * 256, 256)
            result = jnp.dot(tt[...], xk[:, pl.ds(col, 256)], preferred_element_type=F32)
            for i in range(2):
                c = cq * CQ + 2 * cb + i
                flipped = result[:, i * 128:i * 128 + 128].T
                for g in range(SEG):
                    part = flipped[32 * g:32 * g + 32]
                    share[g, c] = part.astype(BF)

                    @pl.when(seg == g)
                    def _():
                        mine[c] = part

            return 0

        lax.fori_loop(0, CQ // 2, lags, 0)
        for d in (2, 1, 3):
            exchange(cq, d).start()
        return 0

    lax.fori_loop(0, NQ, quarter, 0)

    scale = 1.0 / math.sqrt(NF * WIN * SEG)

    def finish(block4, _):
        for d in (1, 2, 3):
            exchange(block4, d).wait_recv()
        c0 = pl.multiple_of(block4 * CQ, CQ)
        total = mine[pl.ds(c0, CQ)]
        for d in (1, 2, 3):
            total = total + landed[d - 1, pl.ds(c0, CQ)].astype(F32)
        out_ref[pl.ds(c0, CQ)] = total * scale
        return 0

    lax.fori_loop(0, NQ, finish, 0)

    for ch in range(NC):
        for ri in halves:
            for d in (1, 2, 3):
                first(ch, ri, d).wait_send()
            for way in (0, 1):
                second(ch, ri, way).wait_send()
                third(ch, ri, way).wait_send()
            fourth(ch, ri).wait_send()

    def sent(block4, _):
        for d in (1, 2, 3):
            exchange(block4, d).wait_send()
        return 0

    lax.fori_loop(0, NQ, sent, 0)


def cross(a, b, tables):
    _, (cb, sb), (la, ls), _ = tables
    vmem = pl.BlockSpec(memory_space=pltpu.VMEM)
    hbm = pl.BlockSpec(memory_space=pl.ANY)
    dma = pltpu.SemaphoreType.DMA
    return pl.pallas_call(
        cross_kernel,
        out_shape=jax.ShapeDtypeStruct((CH, VS // SEG, LAGS), F32),
        in_specs=[hbm, hbm] + [vmem] * 4,
        out_specs=vmem,
        scratch_shapes=[
            pltpu.VMEM((NKB * 16, 2, CH // 8, 8, 128), F32),
            pltpu.VMEM((NC, 2, 2, 4, 4, ROWS_SRC, CL), BF),
            pltpu.VMEM((NKB * 16, VS, 256), BF),
            pltpu.VMEM((2 * NF, CQ * VS), BF),
            pltpu.VMEM((LAGS, 2 * NF), BF),
            pltpu.VMEM((CH, VS // SEG, LAGS), F32),
            pltpu.VMEM((SEG, CH, VS // SEG, LAGS), BF),
            pltpu.VMEM((SEG - 1, CH, VS // SEG, LAGS), BF),
            dma((NC * 6,)), dma((NC * 6,)),
            dma((NC * 4,)), dma((NC * 4,)),
            dma((NC * 4,)), dma((NC * 4,)),
            dma((NC * 2,)), dma((NC * 2,)),
            dma((SEG - 1, NQ)), dma((SEG - 1, NQ)),
            dma((1 + NC * 2,)),
        ],
        compiler_params=pltpu.CompilerParams(
            collective_id=1, has_side_effects=True, vmem_limit_bytes=60 * 1024 * 1024
        ),
        name="cross",
    )(a, b, la, ls, cb, sb)


def on_device(strain_rate, window_length, source_channel):
    tables = jax.tree.map(jnp.asarray, small_tables())
    a, b = spectra(strain_rate, window_length, source_channel, tables)
    return cross(a, b, tables)


def solution(mesh):
    in_specs = (P("seg", None, "chan"), P("seg"), P())
    out_specs = P("chan", "seg", None)
    return jax.shard_map(
        on_device, mesh=mesh, in_specs=in_specs, out_specs=out_specs, check_vma=False
    )
```

```python
import math

import jax
import jax.numpy as jnp
import numpy as np
from jax import lax
from jax.experimental import pallas as pl
from jax.experimental.pallas import tpu as pltpu
from jax.sharding import PartitionSpec as P

W = 4096
NF = 1152
FIRST_BIN = 16
SMOOTH = 64
MAXLAG = 256
LAGS = 512
VS = 128
CHAN = 32
SEG = 4
WIN = 12
CH = 32
NKB = NF // 128
ROWS_MAIN = WIN * CH
ROWS_SRC = 48
ROWS = ROWS_MAIN + ROWS_SRC
GROUPS = (8, 8, 8, 4, 4)
MESH = pl.DeviceIdType.MESH
BF = jnp.bfloat16
F32 = jnp.float32


def unit(product):
    phase = np.mod(product, W).astype(np.float64) * (2.0 * math.pi / W)
    return np.cos(phase).astype(np.float32), np.sin(phase).astype(np.float32)


def small_tables():
    freqs = FIRST_BIN + np.arange(NF)
    coarse = unit(64 * np.arange(64)[:, None] * freqs[None, :128])
    fine = unit(np.arange(64)[:, None] * freqs[None, :])
    lag_coarse = unit(64 * (np.arange(8)[:, None] - 4) * freqs[None, :128])
    width = np.abs(np.arange(NF)[:, None] - np.arange(NF)[None, :]) <= SMOOTH
    inverse = (1.0 / width.sum(axis=0)).astype(np.float32).reshape(1, NF)
    return coarse, fine, lag_coarse, inverse


def slot_masks(rows):
    lane = lax.broadcasted_iota(jnp.int32, (rows, 128), 1)
    return [((lane // 8) // (1 << b)) % 2 == 1 for b in range(4)]


def interleave(values, masks):
    zero = jnp.zeros_like(values[0])
    state = [pltpu.roll(v, 8 * w, 1) if w else v for w, v in enumerate(values)]
    state = state + [zero] * (16 - len(state))
    for b in range(4):
        state = [
            jnp.where(masks[b], state[(i + (1 << b)) % 16], state[i]) for i in range(16)
        ]
    return [state[(-m) % 16] for m in range(16)]


def whiten(acc, first_row, rows, magp, inv_ref):
    span = slice(first_row, first_row + rows)
    magp[:, 0:128] = jnp.zeros((rows, 128), BF)
    magp[:, NF + 128:NF + 256] = jnp.zeros((rows, 128), BF)
    for kb in range(NKB):
        re = acc[span, kb * 128:kb * 128 + 128]
        im = acc[span, NF + kb * 128:NF + kb * 128 + 128]
        magp[:, kb * 128 + 128:kb * 128 + 256] = jnp.sqrt(re * re + im * im).astype(BF)
    band = (
        jnp.abs(
            lax.broadcasted_iota(jnp.int32, (384, 128), 0)
            - 128
            - lax.broadcasted_iota(jnp.int32, (384, 128), 1)
        )
        <= SMOOTH
    ).astype(F32).astype(BF)

    def scale(kb, _):
        col = pl.multiple_of(kb * 128, 128)
        col2 = pl.multiple_of(NF + col, 128)
        total = jnp.dot(magp[:, pl.ds(col, 384)], band, preferred_element_type=F32)
        factor = 1.0 / (total * inv_ref[:, pl.ds(col, 128)] + 1e-06)
        acc[span, pl.ds(col, 128)] = acc[span, pl.ds(col, 128)] * factor
        acc[span, pl.ds(col2, 128)] = acc[span, pl.ds(col2, 128)] * factor
        return 0

    lax.fori_loop(0, NKB, scale, 0)


def spectra_kernel(
    x_ref, wl_ref, sc_ref, ca_ref, sa_ref, cb_ref, sb_ref, inv_ref,
    a_out, b_out,
    xv, xs, rm, rs, tab, lhs, acc, magp,
    ssem, rsem, ssem2, rsem2, lsem,
):
    me = lax.axis_index("chan")
    core = lax.rem(me, 2)
    load = pltpu.make_async_copy(x_ref, xv, lsem.at[0])
    load.start()
    barrier = pltpu.get_barrier_semaphore()

    def greet(d, _):
        pl.semaphore_signal(
            barrier, inc=1, device_id={"chan": lax.rem(me + d, CHAN)}, device_id_type=MESH
        )
        return 0

    lax.fori_loop(1, CHAN, greet, 0)
    pl.semaphore_wait(barrier, CHAN - 1)

    def sender(d):
        return lax.rem(me + CHAN * 13 - 13 * d, CHAN)

    def main_copy(d):
        peer = lax.rem(me + 13 * d, CHAN)
        return pltpu.make_async_remote_copy(
            src_ref=x_ref.at[:, pl.ds(peer * CH, CH), :],
            dst_ref=rm.at[d],
            send_sem=ssem.at[d],
            recv_sem=rsem.at[d],
            device_id={"chan": peer},
            device_id_type=MESH,
        )

    def src_copy(d):
        peer = lax.rem(me + 13 * d, CHAN)
        return pltpu.make_async_remote_copy(
            src_ref=xs.at[peer],
            dst_ref=rs.at[d],
            send_sem=ssem2.at[d],
            recv_sem=rsem2.at[d],
            device_id={"chan": peer},
            device_id_type=MESH,
        )

    def send(d, _):
        main_copy(d).start()
        return 0

    lax.fori_loop(1, 8, send, 0)
    own = pltpu.make_async_copy(x_ref.at[:, pl.ds(me * CH, CH), :], rm.at[0], lsem.at[1])
    own.start()

    load.wait()
    chosen = jnp.broadcast_to(sc_ref[...].astype(F32), (VS, VS)).T
    channel = lax.broadcasted_iota(jnp.int32, (VS, VS), 1).astype(F32)
    hot = jnp.concatenate(
        [(channel + 128.0 * b == chosen).astype(F32).astype(BF) for b in range(CHAN * CH // VS)],
        axis=1,
    )

    def pick(pair, _):
        first = jnp.dot(hot, xv[2 * pair], preferred_element_type=F32)
        second = jnp.dot(hot, xv[2 * pair + 1], preferred_element_type=F32)
        half = pair // 3
        row = pl.multiple_of(lax.rem(pair, 3) * 16, 16)
        for q in range(16):
            both = jnp.concatenate([first[8 * q:8 * q + 8], second[8 * q:8 * q + 8]], axis=0)
            xs[2 * q + half, pl.ds(row, 16), :] = both.astype(BF)
        return 0

    lax.fori_loop(0, WIN // 2, pick, 0)

    def send_src(d, _):
        src_copy(d).start()
        return 0

    lax.fori_loop(1, CHAN, send_src, 0)
    lax.fori_loop(8, CHAN, send, 0)
    own2 = pltpu.make_async_copy(xs.at[me], rs.at[0], lsem.at[2])
    own2.start()

    def make_rows(a, _):
        row = pl.multiple_of(a * 64, 64)
        ca = jnp.broadcast_to(ca_ref[pl.ds(a, 1), :], (64, 128))
        sa = jnp.broadcast_to(sa_ref[pl.ds(a, 1), :], (64, 128))
        for kb in range(NKB):
            cb = cb_ref[:, kb * 128:kb * 128 + 128]
            sb = sb_ref[:, kb * 128:kb * 128 + 128]
            tab[pl.ds(row, 64), kb * 128:kb * 128 + 128] = (ca * cb - sa * sb).astype(BF)
            tab[pl.ds(row, 64), NF + kb * 128:NF + kb * 128 + 128] = (
                -(sa * cb + ca * sb)
            ).astype(BF)
        return 0

    lax.fori_loop(0, 64, make_rows, 0)

    lane = lax.broadcasted_iota(jnp.int32, (1, 128), 1)

    def arrive(d, _):
        main_copy(d).wait_recv()
        src_copy(d).wait_recv()
        return 0

    begin = 0
    for size in GROUPS:
        if begin == 0:
            own.wait()
            own2.wait()
        lax.fori_loop(max(begin, 1), begin + size, arrive, 0)
        for i in range(size):
            d = begin + i
            j = sender(d)

            def keep(w):
                inside = lane + j * 128 < wl_ref[w]
                return jnp.where(inside, 1.0, 0.0)

            for w in range(WIN):
                lhs[w * CH:(w + 1) * CH, i * 128:(i + 1) * 128] = rm[d, w] * keep(w).astype(BF)
            for t in range(3):
                upper = jnp.broadcast_to(keep(core * 6 + 2 * t), (8, 128))
                lower = jnp.broadcast_to(keep(core * 6 + 2 * t + 1), (8, 128))
                both = jnp.concatenate([upper, lower], axis=0).astype(BF)
                lhs[ROWS_MAIN + 16 * t:ROWS_MAIN + 16 * t + 16, i * 128:(i + 1) * 128] = (
                    rs[d, 16 * t:16 * t + 16, :] * both
                )

        def column(ct, _, begin=begin, size=size):
            col = pl.multiple_of(ct * 256, 256)
            right = jnp.concatenate(
                [
                    tab[pl.ds(pl.multiple_of(sender(begin + i) * 128, 128), 128), pl.ds(col, 256)]
                    for i in range(size)
                ],
                axis=0,
            )
            part = jnp.dot(lhs[:, :size * 128], right, preferred_element_type=F32)
            if begin:
                part = part + acc[:, pl.ds(col, 256)]
            acc[:, pl.ds(col, 256)] = part
            return 0

        lax.fori_loop(0, 2 * NF // 256, column, 0)
        begin += size

    out = pltpu.make_async_copy(acc.at[0:ROWS_MAIN], a_out, lsem.at[3])
    out.start()

    def sent(d, _):
        main_copy(d).wait_send()
        src_copy(d).wait_send()
        return 0

    lax.fori_loop(1, CHAN, sent, 0)

    whiten(acc, ROWS_MAIN, ROWS_SRC, magp, inv_ref)
    b_out[...] = acc[ROWS_MAIN:, :].astype(BF)
    out.wait()


def spectra(x, wl, sc, tables):
    (ca, sa), (cb, sb), _, inverse = tables
    vmem = pl.BlockSpec(memory_space=pltpu.VMEM)
    return pl.pallas_call(
        spectra_kernel,
        out_shape=(
            jax.ShapeDtypeStruct((ROWS_MAIN, 2 * NF), F32),
            jax.ShapeDtypeStruct((ROWS_SRC, 2 * NF), BF),
        ),
        in_specs=[
            pl.BlockSpec(memory_space=pl.ANY),
            pl.BlockSpec(memory_space=pltpu.SMEM),
            vmem, vmem, vmem, vmem, vmem, vmem,
        ],
        out_specs=(pl.BlockSpec(memory_space=pl.ANY), vmem),
        scratch_shapes=[
            pltpu.VMEM((WIN, CHAN * CH, 128), BF),
            pltpu.VMEM((CHAN, ROWS_SRC, 128), BF),
            pltpu.VMEM((CHAN, WIN, CH, 128), BF),
            pltpu.VMEM((CHAN, ROWS_SRC, 128), BF),
            pltpu.VMEM((W, 2 * NF), BF),
            pltpu.VMEM((ROWS, 1024), BF),
            pltpu.VMEM((ROWS, 2 * NF), F32),
            pltpu.VMEM((ROWS_SRC, NF + 256), BF),
            pltpu.SemaphoreType.DMA((CHAN,)),
            pltpu.SemaphoreType.DMA((CHAN,)),
            pltpu.SemaphoreType.DMA((CHAN,)),
            pltpu.SemaphoreType.DMA((CHAN,)),
            pltpu.SemaphoreType.DMA((4,)),
        ],
        compiler_params=pltpu.CompilerParams(
            collective_id=0, has_side_effects=True, vmem_limit_bytes=60 * 1024 * 1024
        ),
        name="spectra",
    )(x, wl, sc.reshape(1, VS), ca, sa, cb, sb, inverse)


NC = 3
CKB = NKB // NC
CL = CKB * 128
NQ = 2
CQ = CH // NQ
PC = 4
PARTS = CH // PC


def cross_kernel(
    a_hbm, b_hbm, la_ref, ls_ref, cb_ref, sb_ref, inv_ref, out_ref,
    spec, magp, a_ref, g_ref, bi, xk, tt, share, landed, hop,
    s1, r1, s2, r2, s3, r3, s4, r4, sx, rx, lsem,
):
    me = lax.axis_index("chan")
    seg = lax.axis_index("seg")
    z, y, core = me // 8, lax.rem(me // 2, 4), lax.rem(me, 2)
    load = pltpu.make_async_copy(a_hbm, spec, lsem.at[0])
    load.start()

    def at(zz, yy, cc):
        return {"chan": lax.rem(zz + 4, 4) * 8 + lax.rem(yy + 4, 4) * 2 + cc}

    def beyond(axis, d):
        return at(z + d, y, core) if axis == 0 else at(z, y + d, core)

    def segment(d):
        return {"seg": lax.rem(seg + d, SEG)}

    barrier = pltpu.get_barrier_semaphore()
    for d in (1, 2, 3):
        for who in (beyond(0, d), beyond(1, d), segment(d)):
            pl.semaphore_signal(barrier, inc=1, device_id=who, device_id_type=MESH)
    pl.semaphore_signal(barrier, inc=1, device_id=at(z, y, 1 - core), device_id_type=MESH)
    pl.semaphore_wait(barrier, 10)

    def remote(src, dst, send, recv, who):
        return pltpu.make_async_remote_copy(
            src_ref=src, dst_ref=dst, send_sem=send, recv_sem=recv, device_id=who, device_id_type=MESH
        )

    def block(ch, ri):
        return b_hbm.at[:, ri * NF + ch * CL:ri * NF + (ch + 1) * CL]

    def first(ch, ri, d):
        k = (ch * 2 + ri) * 3 + d - 1
        return remote(block(ch, ri), g_ref.at[ch, ri, core, z, y], s1.at[k], r1.at[k], beyond(ri, d))

    def line(ch, ri, start, size, d):
        if ri == 0:
            return g_ref.at[ch, ri, core, start:start + size, lax.rem(y + d + 4, 4)]
        return g_ref.at[ch, ri, core, lax.rem(z + d + 4, 4), start:start + size]

    def second(ch, ri, way):
        k = (ch * 2 + ri) * 2 + way
        d = 1 if way == 0 else 3
        whole = line(ch, ri, 0, 4, 0)
        return remote(whole, whole, s2.at[k], r2.at[k], beyond(1 - ri, d))

    def third(ch, ri, way):
        k = (ch * 2 + ri) * 2 + way
        d = 1 if way == 0 else 3
        part = line(ch, ri, 2 * way, 2, -1 if way == 0 else 1)
        return remote(part, part, s3.at[k], r3.at[k], beyond(1 - ri, d))

    def fourth(ch, ri):
        k = ch * 2 + ri
        part = g_ref.at[ch, ri, core]
        return remote(part, part, s4.at[k], r4.at[k], at(z, y, 1 - core))

    def own(ch, ri):
        return pltpu.make_async_copy(block(ch, ri), g_ref.at[ch, ri, core, z, y], lsem.at[1 + ch * 2 + ri])

    halves = (0, 1)
    for ch in range(NC):
        for ri in halves:
            for d in (2, 1, 3):
                first(ch, ri, d).start()
            own(ch, ri).start()

    for a in range(8):
        ca = jnp.broadcast_to(la_ref[a:a + 1, :], (64, 128))
        sa = jnp.broadcast_to(ls_ref[a:a + 1, :], (64, 128))
        for kb in range(NKB):
            cols = slice(kb * 128, kb * 128 + 128)
            cols2 = slice(NF + kb * 128, NF + kb * 128 + 128)
            cb, sb = cb_ref[:, cols], sb_ref[:, cols]
            tt[a * 64:a * 64 + 64, cols] = (ca * cb - sa * sb).astype(BF)
            tt[a * 64:a * 64 + 64, cols2] = (-(sa * cb + ca * sb)).astype(BF)

    masks = slot_masks(8)
    diagonal = (
        lax.rem(lax.broadcasted_iota(jnp.int32, (8, 128), 1), 8)
        == lax.broadcasted_iota(jnp.int32, (8, 128), 0)
    )

    def step_second(ch):
        for ri in halves:
            for d in (1, 2, 3):
                first(ch, ri, d).wait_recv()
            own(ch, ri).wait()
            for way in (0, 1):
                second(ch, ri, way).start()

    def step_third(ch):
        for ri in halves:
            for way in (0, 1):
                second(ch, ri, way).wait_recv()
                third(ch, ri, way).start()

    def step_fourth(ch):
        for ri in halves:
            for way in (0, 1):
                third(ch, ri, way).wait_recv()
            fourth(ch, ri).start()

    def arrived(ch):
        for ri in halves:
            fourth(ch, ri).wait_recv()

    def bins(ch, kbl):
        kb = ch * CKB + kbl

        def spread(qq, _):
            row = pl.multiple_of(qq * 16, 16)
            for ri in range(2):
                col = kbl * 128
                outs = []
                for q2 in range(2):
                    q = 2 * qq + q2
                    values = []
                    for half in range(2):
                        for t in range(3):
                            pair = g_ref[
                                ch, ri, half, q // 4, lax.rem(q, 4), 16 * t:16 * t + 16, col:col + 128
                            ].astype(F32)
                            values += [pair[:8], pair[8:]]
                    outs.append(interleave(values, masks))
                for m in range(16):
                    both = jnp.concatenate([outs[0][m], outs[1][m]], axis=0)
                    bi[kb * 16 + m, pl.ds(row, 16), ri * 128:ri * 128 + 128] = both.astype(BF)
            return 0

        lax.fori_loop(0, 8, spread, 0)

    def products(cq):
        def several(it, _):
            for p in range(NQ):
                mp = it * NQ + p
                results = []
                for half in range(2):
                    group = 2 * mp + half
                    sides = []
                    for ri in range(2):
                        tiles = [
                            jnp.where(
                                diagonal,
                                jnp.broadcast_to(
                                    a_ref[group, ri, cq * (CQ // 8) + c // 8, c % 8:c % 8 + 1, :], (8, 128)
                                ),
                                0.0,
                            )
                            for c in range(CQ)
                        ]
                        sides.append(jnp.concatenate(tiles, axis=0).astype(BF))
                    left = jnp.concatenate(sides, axis=1)
                    bre = bi[group, :, 0:128]
                    bim = bi[group, :, 128:256]
                    right = jnp.concatenate(
                        [
                            jnp.concatenate([bre, bim], axis=1),
                            jnp.concatenate([-bim, bre], axis=1),
                        ],
                        axis=0,
                    )
                    results.append(
                        lax.dot_general(
                            left, right, (((1,), (1,)), ((), ())), preferred_element_type=F32
                        )
                    )
                row = pl.multiple_of(mp * 16, 16)
                for ri in range(2):
                    for c in range(CQ):
                        both = jnp.concatenate(
                            [r[c * 8:c * 8 + 8, ri * 128:ri * 128 + 128] for r in results], axis=0
                        )
                        xk[pl.ds(pl.multiple_of(ri * NF + row, 16), 16), c * 128:c * 128 + 128] = both.astype(BF)
            return 0

        lax.fori_loop(0, NKB * 8 // NQ, several, 0)

    def spread_own(step, _):
        kb = step // 2
        for part in range(2):
            c8 = pl.multiple_of(lax.rem(step, 2) * 16 + part * 8, 8)
            for ri in range(2):
                col = pl.multiple_of(ri * NF + kb * 128, 128)
                values = [
                    spec[pl.ds(pl.multiple_of(w * CH + c8, 8), 8), pl.ds(col, 128)] for w in range(WIN)
                ]
                for m, value in enumerate(interleave(values, masks)):
                    a_ref[kb * 16 + m, ri, lax.rem(step, 2) * 2 + part] = value
        return 0

    for ch in range(NC):
        step_second(ch)
    load.wait()
    whiten(spec, 0, ROWS_MAIN, magp, inv_ref)
    step_third(0)
    step_third(1)
    lax.fori_loop(0, 6, spread_own, 0)
    step_third(2)
    step_fourth(0)
    lax.fori_loop(6, 12, spread_own, 0)
    step_fourth(1)
    lax.fori_loop(12, NKB * 2, spread_own, 0)
    arrived(0)
    bins(0, 0)
    step_fourth(2)
    bins(0, 1)
    bins(0, 2)
    for ch in range(1, NC):
        arrived(ch)
        for kbl in range(CKB):
            bins(ch, kbl)

    half = PC // 2

    def chans(part, h):
        return pl.ds(pl.multiple_of(part * PC + h * half, half), half)

    def outward(part, way):
        return remote(
            share.at[lax.rem(seg + 2, SEG), chans(part, way)], hop.at[way, part],
            sx.at[way, part], rx.at[way, part], segment(1 if way == 0 else 3),
        )

    def direct(part, way):
        return remote(
            share.at[lax.rem(seg + (1 if way == 0 else 3), SEG), chans(part, 1 - way)],
            landed.at[way, chans(part, 1 - way)],
            sx.at[2 + way, part], rx.at[2 + way, part], segment(1 if way == 0 else 3),
        )

    def joint(part, way):
        return remote(
            share.at[lax.rem(seg + (1 if way == 0 else 3), SEG), chans(part, way)],
            landed.at[way, chans(part, way)],
            sx.at[4 + way, part], rx.at[4 + way, part], segment(1 if way == 0 else 3),
        )

    def pass_on(part):
        for way in (0, 1):
            outward(part, way).wait_recv()
            to = lax.rem(seg + (1 if way == 0 else 3), SEG)
            total = share[to, chans(part, way)].astype(F32) + hop[way, part].astype(F32)
            share[to, chans(part, way)] = total.astype(BF)
            joint(part, way).start()

    def quarter(cq, _):
        products(cq)

        def lags(local, _):
            part = cq * (CQ // PC) + local
            for pair in range(PC // 2):
                col = pl.multiple_of(local * PC * VS + pair * 256, 256)
                result = jnp.dot(tt[...], xk[:, pl.ds(col, 256)], preferred_element_type=F32)
                for i in range(2):
                    c = part * PC + 2 * pair + i
                    flipped = result[:, i * 128:i * 128 + 128].T
                    for g in range(SEG):
                        piece = flipped[32 * g:32 * g + 32]
                        share[g, c] = piece.astype(BF)

                        @pl.when(seg == g)
                        def _():
                            out_ref[c] = piece

            for way in (0, 1):
                outward(part, way).start()
            for way in (0, 1):
                direct(part, way).start()

            @pl.when(part > 0)
            def _():
                pass_on(part - 1)

            return 0

        lax.fori_loop(0, CQ // PC, lags, 0)
        return 0

    lax.fori_loop(0, NQ, quarter, 0)

    pass_on(PARTS - 1)

    def finish(part, _):
        for way in (0, 1):
            direct(part, way).wait_recv()
            joint(part, way).wait_recv()
        c0 = pl.multiple_of(part * PC, PC)
        total = out_ref[pl.ds(c0, PC)]
        for way in (0, 1):
            total = total + landed[way, pl.ds(c0, PC)].astype(F32)
        out_ref[pl.ds(c0, PC)] = total
        return 0

    lax.fori_loop(0, PARTS, finish, 0)

    for ch in range(NC):
        for ri in halves:
            for d in (1, 2, 3):
                first(ch, ri, d).wait_send()
            for way in (0, 1):
                second(ch, ri, way).wait_send()
                third(ch, ri, way).wait_send()
            fourth(ch, ri).wait_send()

    def sent(part, _):
        for way in (0, 1):
            outward(part, way).wait_send()
            direct(part, way).wait_send()
            joint(part, way).wait_send()
        return 0

    lax.fori_loop(0, PARTS, sent, 0)


def cross(a, b, tables):
    _, (cb, sb), (la, ls), inverse = tables
    vmem = pl.BlockSpec(memory_space=pltpu.VMEM)
    hbm = pl.BlockSpec(memory_space=pl.ANY)
    dma = pltpu.SemaphoreType.DMA
    return pl.pallas_call(
        cross_kernel,
        out_shape=jax.ShapeDtypeStruct((CH, VS // SEG, LAGS), F32),
        in_specs=[hbm, hbm] + [vmem] * 5,
        out_specs=vmem,
        scratch_shapes=[
            pltpu.VMEM((ROWS_MAIN, 2 * NF), F32),
            pltpu.VMEM((ROWS_MAIN, NF + 256), BF),
            pltpu.VMEM((NKB * 16, 2, CH // 8, 8, 128), F32),
            pltpu.VMEM((NC, 2, 2, 4, 4, ROWS_SRC, CL), BF),
            pltpu.VMEM((NKB * 16, VS, 256), BF),
            pltpu.VMEM((2 * NF, CQ * VS), BF),
            pltpu.VMEM((LAGS, 2 * NF), BF),
            pltpu.VMEM((SEG, CH, VS // SEG, LAGS), BF),
            pltpu.VMEM((2, CH, VS // SEG, LAGS), BF),
            pltpu.VMEM((2, PARTS, PC // 2, VS // SEG, LAGS), BF),
            dma((NC * 6,)), dma((NC * 6,)),
            dma((NC * 4,)), dma((NC * 4,)),
            dma((NC * 4,)), dma((NC * 4,)),
            dma((NC * 2,)), dma((NC * 2,)),
            dma((6, PARTS)), dma((6, PARTS)),
            dma((1 + NC * 2,)),
        ],
        compiler_params=pltpu.CompilerParams(
            collective_id=1, has_side_effects=True, vmem_limit_bytes=60 * 1024 * 1024
        ),
        name="cross",
    )(a, b, la, ls, cb, sb, inverse)


def on_device(strain_rate, window_length, source_channel):
    tables = jax.tree.map(jnp.asarray, small_tables())
    a, b = spectra(strain_rate, window_length, source_channel, tables)
    return cross(a, b, tables) * (1.0 / math.sqrt(NF * WIN * SEG))


def solution(mesh):
    in_specs = (P("seg", None, "chan"), P("seg"), P())
    out_specs = P("chan", "seg", None)
    return jax.shard_map(
        on_device, mesh=mesh, in_specs=in_specs, out_specs=out_specs, check_vma=False
    )
```

```python
import math

import jax
import jax.numpy as jnp
import numpy as np
from jax import lax
from jax.experimental import pallas as pl
from jax.experimental.pallas import tpu as pltpu
from jax.sharding import PartitionSpec as P

W = 4096
NF = 1152
FIRST_BIN = 16
SMOOTH = 64
MAXLAG = 256
LAGS = 512
VS = 128
CHAN = 32
SEG = 4
WIN = 12
CH = 32
NKB = NF // 128
ROWS_MAIN = WIN * CH
ROWS_SRC = 48
ROWS = ROWS_MAIN + ROWS_SRC
GROUPS = (8, 8, 8, 4, 4)
MESH = pl.DeviceIdType.MESH
BF = jnp.bfloat16
F32 = jnp.float32


def unit(product):
    phase = np.mod(product, W).astype(np.float64) * (2.0 * math.pi / W)
    return np.cos(phase).astype(np.float32), np.sin(phase).astype(np.float32)


def small_tables():
    freqs = FIRST_BIN + np.arange(NF)
    coarse = unit(64 * np.arange(64)[:, None] * freqs[None, :128])
    fine = unit(np.arange(64)[:, None] * freqs[None, :])
    lag_coarse = unit(64 * (np.arange(8)[:, None] - 4) * freqs[None, :128])
    width = np.abs(np.arange(NF)[:, None] - np.arange(NF)[None, :]) <= SMOOTH
    inverse = (1.0 / width.sum(axis=0)).astype(np.float32).reshape(1, NF)
    return coarse, fine, lag_coarse, inverse


def slot_masks(rows):
    lane = lax.broadcasted_iota(jnp.int32, (rows, 128), 1)
    return [((lane // 8) // (1 << b)) % 2 == 1 for b in range(4)]


def interleave(values, masks):
    zero = jnp.zeros_like(values[0])
    state = [pltpu.roll(v, 8 * w, 1) if w else v for w, v in enumerate(values)]
    state = state + [zero] * (16 - len(state))
    for b in range(4):
        state = [
            jnp.where(masks[b], state[(i + (1 << b)) % 16], state[i]) for i in range(16)
        ]
    return [state[(-m) % 16] for m in range(16)]


def whiten(acc, first_row, rows, magp, inv_ref):
    span = slice(first_row, first_row + rows)
    magp[:, 0:128] = jnp.zeros((rows, 128), BF)
    magp[:, NF + 128:NF + 256] = jnp.zeros((rows, 128), BF)
    for kb in range(NKB):
        re = acc[span, kb * 128:kb * 128 + 128]
        im = acc[span, NF + kb * 128:NF + kb * 128 + 128]
        magp[:, kb * 128 + 128:kb * 128 + 256] = jnp.sqrt(re * re + im * im).astype(BF)
    band = (
        jnp.abs(
            lax.broadcasted_iota(jnp.int32, (384, 128), 0)
            - 128
            - lax.broadcasted_iota(jnp.int32, (384, 128), 1)
        )
        <= SMOOTH
    ).astype(F32).astype(BF)

    def scale(kb, _):
        col = pl.multiple_of(kb * 128, 128)
        col2 = pl.multiple_of(NF + col, 128)
        total = jnp.dot(magp[:, pl.ds(col, 384)], band, preferred_element_type=F32)
        factor = 1.0 / (total * inv_ref[:, pl.ds(col, 128)] + 1e-06)
        acc[span, pl.ds(col, 128)] = acc[span, pl.ds(col, 128)] * factor
        acc[span, pl.ds(col2, 128)] = acc[span, pl.ds(col2, 128)] * factor
        return 0

    lax.fori_loop(0, NKB, scale, 0)


def spectra_kernel(
    x_ref, wl_ref, sc_ref, ca_ref, sa_ref, cb_ref, sb_ref, inv_ref,
    a_out, b_out,
    xv, xs, rm, rs, tab, lhs, acc, magp,
    ssem, rsem, ssem2, rsem2, lsem,
):
    me = lax.axis_index("chan")
    core = lax.rem(me, 2)
    load = pltpu.make_async_copy(x_ref, xv, lsem.at[0])
    load.start()
    barrier = pltpu.get_barrier_semaphore()

    def greet(d, _):
        pl.semaphore_signal(
            barrier, inc=1, device_id={"chan": lax.rem(me + d, CHAN)}, device_id_type=MESH
        )
        return 0

    lax.fori_loop(1, CHAN, greet, 0)
    pl.semaphore_wait(barrier, CHAN - 1)

    def sender(d):
        return lax.rem(me + CHAN * 13 - 13 * d, CHAN)

    def main_copy(d):
        peer = lax.rem(me + 13 * d, CHAN)
        return pltpu.make_async_remote_copy(
            src_ref=x_ref.at[:, pl.ds(peer * CH, CH), :],
            dst_ref=rm.at[d],
            send_sem=ssem.at[d],
            recv_sem=rsem.at[d],
            device_id={"chan": peer},
            device_id_type=MESH,
        )

    def src_copy(d):
        peer = lax.rem(me + 13 * d, CHAN)
        return pltpu.make_async_remote_copy(
            src_ref=xs.at[peer],
            dst_ref=rs.at[d],
            send_sem=ssem2.at[d],
            recv_sem=rsem2.at[d],
            device_id={"chan": peer},
            device_id_type=MESH,
        )

    def send(d, _):
        main_copy(d).start()
        return 0

    lax.fori_loop(1, 8, send, 0)
    own = pltpu.make_async_copy(x_ref.at[:, pl.ds(me * CH, CH), :], rm.at[0], lsem.at[1])
    own.start()

    load.wait()
    chosen = jnp.broadcast_to(sc_ref[...].astype(F32), (VS, VS)).T
    channel = lax.broadcasted_iota(jnp.int32, (VS, VS), 1).astype(F32)
    hot = jnp.concatenate(
        [(channel + 128.0 * b == chosen).astype(F32).astype(BF) for b in range(CHAN * CH // VS)],
        axis=1,
    )

    def pick(pair, _):
        first = jnp.dot(hot, xv[2 * pair], preferred_element_type=F32)
        second = jnp.dot(hot, xv[2 * pair + 1], preferred_element_type=F32)
        half = pair // 3
        row = pl.multiple_of(lax.rem(pair, 3) * 16, 16)
        for q in range(16):
            both = jnp.concatenate([first[8 * q:8 * q + 8], second[8 * q:8 * q + 8]], axis=0)
            xs[2 * q + half, pl.ds(row, 16), :] = both.astype(BF)
        return 0

    lax.fori_loop(0, WIN // 2, pick, 0)

    def send_src(d, _):
        src_copy(d).start()
        return 0

    lax.fori_loop(1, CHAN, send_src, 0)
    lax.fori_loop(8, CHAN, send, 0)
    own2 = pltpu.make_async_copy(xs.at[me], rs.at[0], lsem.at[2])
    own2.start()

    def make_rows(a, _):
        row = pl.multiple_of(a * 64, 64)
        ca = jnp.broadcast_to(ca_ref[pl.ds(a, 1), :], (64, 128))
        sa = jnp.broadcast_to(sa_ref[pl.ds(a, 1), :], (64, 128))
        for kb in range(NKB):
            cb = cb_ref[:, kb * 128:kb * 128 + 128]
            sb = sb_ref[:, kb * 128:kb * 128 + 128]
            tab[pl.ds(row, 64), kb * 128:kb * 128 + 128] = (ca * cb - sa * sb).astype(BF)
            tab[pl.ds(row, 64), NF + kb * 128:NF + kb * 128 + 128] = (
                -(sa * cb + ca * sb)
            ).astype(BF)
        return 0

    lax.fori_loop(0, 64, make_rows, 0)

    lane = lax.broadcasted_iota(jnp.int32, (1, 128), 1)

    def arrive(d, _):
        main_copy(d).wait_recv()
        src_copy(d).wait_recv()
        return 0

    begin = 0
    for size in GROUPS:
        if begin == 0:
            own.wait()
            own2.wait()
        lax.fori_loop(max(begin, 1), begin + size, arrive, 0)
        for i in range(size):
            d = begin + i
            j = sender(d)

            def keep(w):
                inside = lane + j * 128 < wl_ref[w]
                return jnp.where(inside, 1.0, 0.0)

            for w in range(WIN):
                lhs[w * CH:(w + 1) * CH, i * 128:(i + 1) * 128] = rm[d, w] * keep(w).astype(BF)
            for t in range(3):
                upper = jnp.broadcast_to(keep(core * 6 + 2 * t), (8, 128))
                lower = jnp.broadcast_to(keep(core * 6 + 2 * t + 1), (8, 128))
                both = jnp.concatenate([upper, lower], axis=0).astype(BF)
                lhs[ROWS_MAIN + 16 * t:ROWS_MAIN + 16 * t + 16, i * 128:(i + 1) * 128] = (
                    rs[d, 16 * t:16 * t + 16, :] * both
                )

        def column(ct, _, begin=begin, size=size):
            col = pl.multiple_of(ct * 256, 256)
            right = jnp.concatenate(
                [
                    tab[pl.ds(pl.multiple_of(sender(begin + i) * 128, 128), 128), pl.ds(col, 256)]
                    for i in range(size)
                ],
                axis=0,
            )
            part = jnp.dot(lhs[:, :size * 128], right, preferred_element_type=F32)
            if begin:
                part = part + acc[:, pl.ds(col, 256)]
            acc[:, pl.ds(col, 256)] = part
            return 0

        lax.fori_loop(0, 2 * NF // 256, column, 0)
        begin += size

    out = pltpu.make_async_copy(acc.at[0:ROWS_MAIN], a_out, lsem.at[3])
    out.start()

    def sent(d, _):
        main_copy(d).wait_send()
        src_copy(d).wait_send()
        return 0

    lax.fori_loop(1, CHAN, sent, 0)

    whiten(acc, ROWS_MAIN, ROWS_SRC, magp, inv_ref)
    b_out[...] = acc[ROWS_MAIN:, :].astype(BF)
    out.wait()


def spectra(x, wl, sc, tables):
    (ca, sa), (cb, sb), _, inverse = tables
    vmem = pl.BlockSpec(memory_space=pltpu.VMEM)
    return pl.pallas_call(
        spectra_kernel,
        out_shape=(
            jax.ShapeDtypeStruct((ROWS_MAIN, 2 * NF), F32),
            jax.ShapeDtypeStruct((ROWS_SRC, 2 * NF), BF),
        ),
        in_specs=[
            pl.BlockSpec(memory_space=pl.ANY),
            pl.BlockSpec(memory_space=pltpu.SMEM),
            vmem, vmem, vmem, vmem, vmem, vmem,
        ],
        out_specs=(pl.BlockSpec(memory_space=pl.ANY), vmem),
        scratch_shapes=[
            pltpu.VMEM((WIN, CHAN * CH, 128), BF),
            pltpu.VMEM((CHAN, ROWS_SRC, 128), BF),
            pltpu.VMEM((CHAN, WIN, CH, 128), BF),
            pltpu.VMEM((CHAN, ROWS_SRC, 128), BF),
            pltpu.VMEM((W, 2 * NF), BF),
            pltpu.VMEM((ROWS, 1024), BF),
            pltpu.VMEM((ROWS, 2 * NF), F32),
            pltpu.VMEM((ROWS_SRC, NF + 256), BF),
            pltpu.SemaphoreType.DMA((CHAN,)),
            pltpu.SemaphoreType.DMA((CHAN,)),
            pltpu.SemaphoreType.DMA((CHAN,)),
            pltpu.SemaphoreType.DMA((CHAN,)),
            pltpu.SemaphoreType.DMA((4,)),
        ],
        compiler_params=pltpu.CompilerParams(
            collective_id=0, has_side_effects=True, vmem_limit_bytes=60 * 1024 * 1024
        ),
        name="spectra",
    )(x, wl, sc.reshape(1, VS), ca, sa, cb, sb, inverse)


NC = 3
CKB = NKB // NC
CL = CKB * 128
NQ = 2
CQ = CH // NQ
PC = 4
STEP = 8
PARTS = CH // PC


def cross_kernel(
    a_hbm, b_hbm, la_ref, ls_ref, cb_ref, sb_ref, inv_ref, out_ref,
    spec, magp, a_ref, g_ref, bi, xk, tt, share, landed, hop,
    s1, r1, s2, r2, s3, r3, s4, r4, sx, rx, lsem,
):
    me = lax.axis_index("chan")
    seg = lax.axis_index("seg")
    z, y, core = me // 8, lax.rem(me // 2, 4), lax.rem(me, 2)
    load = pltpu.make_async_copy(a_hbm, spec, lsem.at[0])
    load.start()

    def at(zz, yy, cc):
        return {"chan": lax.rem(zz + 4, 4) * 8 + lax.rem(yy + 4, 4) * 2 + cc}

    def beyond(axis, d):
        return at(z + d, y, core) if axis == 0 else at(z, y + d, core)

    def segment(d):
        return {"seg": lax.rem(seg + d, SEG)}

    barrier = pltpu.get_barrier_semaphore()
    for d in (1, 2, 3):
        for who in (beyond(0, d), beyond(1, d), segment(d)):
            pl.semaphore_signal(barrier, inc=1, device_id=who, device_id_type=MESH)
    pl.semaphore_signal(barrier, inc=1, device_id=at(z, y, 1 - core), device_id_type=MESH)
    pl.semaphore_wait(barrier, 10)

    def remote(src, dst, send, recv, who):
        return pltpu.make_async_remote_copy(
            src_ref=src, dst_ref=dst, send_sem=send, recv_sem=recv, device_id=who, device_id_type=MESH
        )

    def block(ch, ri):
        return b_hbm.at[:, ri * NF + ch * CL:ri * NF + (ch + 1) * CL]

    def first(ch, ri, d):
        k = (ch * 2 + ri) * 3 + d - 1
        return remote(block(ch, ri), g_ref.at[ch, ri, core, z, y], s1.at[k], r1.at[k], beyond(ri, d))

    def line(ch, ri, start, size, d):
        if ri == 0:
            return g_ref.at[ch, ri, core, start:start + size, lax.rem(y + d + 4, 4)]
        return g_ref.at[ch, ri, core, lax.rem(z + d + 4, 4), start:start + size]

    def second(ch, ri, way):
        k = (ch * 2 + ri) * 2 + way
        d = 1 if way == 0 else 3
        whole = line(ch, ri, 0, 4, 0)
        return remote(whole, whole, s2.at[k], r2.at[k], beyond(1 - ri, d))

    def third(ch, ri, way):
        k = (ch * 2 + ri) * 2 + way
        d = 1 if way == 0 else 3
        part = line(ch, ri, 2 * way, 2, -1 if way == 0 else 1)
        return remote(part, part, s3.at[k], r3.at[k], beyond(1 - ri, d))

    def fourth(ch, ri):
        k = ch * 2 + ri
        part = g_ref.at[ch, ri, core]
        return remote(part, part, s4.at[k], r4.at[k], at(z, y, 1 - core))

    def own(ch, ri):
        return pltpu.make_async_copy(block(ch, ri), g_ref.at[ch, ri, core, z, y], lsem.at[1 + ch * 2 + ri])

    halves = (0, 1)
    for ch in range(NC):
        for ri in halves:
            for d in (2, 1, 3):
                first(ch, ri, d).start()
            own(ch, ri).start()

    for a in range(8):
        ca = jnp.broadcast_to(la_ref[a:a + 1, :], (64, 128))
        sa = jnp.broadcast_to(ls_ref[a:a + 1, :], (64, 128))
        for kb in range(NKB):
            cols = slice(kb * 128, kb * 128 + 128)
            cols2 = slice(NF + kb * 128, NF + kb * 128 + 128)
            cb, sb = cb_ref[:, cols], sb_ref[:, cols]
            tt[a * 64:a * 64 + 64, cols] = (ca * cb - sa * sb).astype(BF)
            tt[a * 64:a * 64 + 64, cols2] = (-(sa * cb + ca * sb)).astype(BF)

    masks = slot_masks(8)
    diagonal = (
        lax.rem(lax.broadcasted_iota(jnp.int32, (8, 128), 1), 8)
        == lax.broadcasted_iota(jnp.int32, (8, 128), 0)
    )

    def step_second(ch):
        for ri in halves:
            for d in (1, 2, 3):
                first(ch, ri, d).wait_recv()
            own(ch, ri).wait()
            for way in (0, 1):
                second(ch, ri, way).start()

    def step_third(ch):
        for ri in halves:
            for way in (0, 1):
                second(ch, ri, way).wait_recv()
                third(ch, ri, way).start()

    def step_fourth(ch):
        for ri in halves:
            for way in (0, 1):
                third(ch, ri, way).wait_recv()
            fourth(ch, ri).start()

    def arrived(ch):
        for ri in halves:
            fourth(ch, ri).wait_recv()

    def bins(ch, kbl):
        kb = ch * CKB + kbl

        def spread(qq, _):
            row = pl.multiple_of(qq * 16, 16)
            for ri in range(2):
                col = kbl * 128
                outs = []
                for q2 in range(2):
                    q = 2 * qq + q2
                    values = []
                    for half in range(2):
                        for t in range(3):
                            pair = g_ref[
                                ch, ri, half, q // 4, lax.rem(q, 4), 16 * t:16 * t + 16, col:col + 128
                            ].astype(F32)
                            values += [pair[:8], pair[8:]]
                    outs.append(interleave(values, masks))
                for m in range(16):
                    both = jnp.concatenate([outs[0][m], outs[1][m]], axis=0)
                    bi[kb * 16 + m, pl.ds(row, 16), ri * 128:ri * 128 + 128] = both.astype(BF)
            return 0

        lax.fori_loop(0, 8, spread, 0)

    def products(cq):
        def several(it, _):
            for p in range(STEP):
                mp = it * STEP + p
                results = []
                for half in range(2):
                    group = 2 * mp + half
                    sides = []
                    for ri in range(2):
                        tiles = [
                            jnp.where(
                                diagonal,
                                jnp.broadcast_to(
                                    a_ref[group, ri, cq * (CQ // 8) + c // 8, c % 8:c % 8 + 1, :], (8, 128)
                                ),
                                0.0,
                            )
                            for c in range(CQ)
                        ]
                        sides.append(jnp.concatenate(tiles, axis=0).astype(BF))
                    left = jnp.concatenate(sides, axis=1)
                    bre = bi[group, :, 0:128]
                    bim = bi[group, :, 128:256]
                    right = jnp.concatenate(
                        [
                            jnp.concatenate([bre, bim], axis=1),
                            jnp.concatenate([-bim, bre], axis=1),
                        ],
                        axis=0,
                    )
                    results.append(
                        lax.dot_general(
                            left, right, (((1,), (1,)), ((), ())), preferred_element_type=F32
                        )
                    )
                row = pl.multiple_of(mp * 16, 16)
                for ri in range(2):
                    for c in range(CQ):
                        both = jnp.concatenate(
                            [r[c * 8:c * 8 + 8, ri * 128:ri * 128 + 128] for r in results], axis=0
                        )
                        xk[pl.ds(pl.multiple_of(ri * NF + row, 16), 16), c * 128:c * 128 + 128] = both.astype(BF)
            return 0

        lax.fori_loop(0, NKB * 8 // STEP, several, 0)

    def spread_own(step, _):
        kb = step // 2
        for part in range(2):
            c8 = pl.multiple_of(lax.rem(step, 2) * 16 + part * 8, 8)
            for ri in range(2):
                col = pl.multiple_of(ri * NF + kb * 128, 128)
                values = [
                    spec[pl.ds(pl.multiple_of(w * CH + c8, 8), 8), pl.ds(col, 128)] for w in range(WIN)
                ]
                for m, value in enumerate(interleave(values, masks)):
                    a_ref[kb * 16 + m, ri, lax.rem(step, 2) * 2 + part] = value
        return 0

    for ch in range(NC):
        step_second(ch)
    load.wait()
    whiten(spec, 0, ROWS_MAIN, magp, inv_ref)
    step_third(0)
    step_third(1)
    lax.fori_loop(0, 6, spread_own, 0)
    step_third(2)
    step_fourth(0)
    lax.fori_loop(6, 12, spread_own, 0)
    step_fourth(1)
    lax.fori_loop(12, NKB * 2, spread_own, 0)
    arrived(0)
    bins(0, 0)
    step_fourth(2)
    bins(0, 1)
    bins(0, 2)
    for ch in range(1, NC):
        arrived(ch)
        for kbl in range(CKB):
            bins(ch, kbl)

    half = PC // 2

    def chans(part, h):
        return pl.ds(pl.multiple_of(part * PC + h * half, half), half)

    def outward(part, way):
        return remote(
            share.at[lax.rem(seg + 2, SEG), chans(part, way)], hop.at[way, part],
            sx.at[way, part], rx.at[way, part], segment(1 if way == 0 else 3),
        )

    def direct(part, way):
        return remote(
            share.at[lax.rem(seg + (1 if way == 0 else 3), SEG), chans(part, 1 - way)],
            landed.at[way, chans(part, 1 - way)],
            sx.at[2 + way, part], rx.at[2 + way, part], segment(1 if way == 0 else 3),
        )

    def joint(part, way):
        return remote(
            share.at[lax.rem(seg + (1 if way == 0 else 3), SEG), chans(part, way)],
            landed.at[way, chans(part, way)],
            sx.at[4 + way, part], rx.at[4 + way, part], segment(1 if way == 0 else 3),
        )

    def pass_on(part):
        for way in (0, 1):
            outward(part, way).wait_recv()
            to = lax.rem(seg + (1 if way == 0 else 3), SEG)
            total = share[to, chans(part, way)].astype(F32) + hop[way, part].astype(F32)
            share[to, chans(part, way)] = total.astype(BF)
            joint(part, way).start()

    def quarter(cq, _):
        products(cq)

        def lags(local, _):
            part = cq * (CQ // PC) + local
            for pair in range(PC // 2):
                col = pl.multiple_of(local * PC * VS + pair * 256, 256)
                result = jnp.dot(tt[...], xk[:, pl.ds(col, 256)], preferred_element_type=F32)
                for i in range(2):
                    c = part * PC + 2 * pair + i
                    flipped = result[:, i * 128:i * 128 + 128].T
                    for g in range(SEG):
                        piece = flipped[32 * g:32 * g + 32]
                        share[g, c] = piece.astype(BF)

                        @pl.when(seg == g)
                        def _():
                            out_ref[c] = piece

            for way in (0, 1):
                outward(part, way).start()
            for way in (0, 1):
                direct(part, way).start()

            @pl.when(part > 0)
            def _():
                pass_on(part - 1)

            return 0

        lax.fori_loop(0, CQ // PC, lags, 0)
        return 0

    lax.fori_loop(0, NQ, quarter, 0)

    pass_on(PARTS - 1)

    def finish(part, _):
        for way in (0, 1):
            direct(part, way).wait_recv()
            joint(part, way).wait_recv()
        c0 = pl.multiple_of(part * PC, PC)
        total = out_ref[pl.ds(c0, PC)]
        for way in (0, 1):
            total = total + landed[way, pl.ds(c0, PC)].astype(F32)
        out_ref[pl.ds(c0, PC)] = total
        return 0

    lax.fori_loop(0, PARTS, finish, 0)

    for ch in range(NC):
        for ri in halves:
            for d in (1, 2, 3):
                first(ch, ri, d).wait_send()
            for way in (0, 1):
                second(ch, ri, way).wait_send()
                third(ch, ri, way).wait_send()
            fourth(ch, ri).wait_send()

    def sent(part, _):
        for way in (0, 1):
            outward(part, way).wait_send()
            direct(part, way).wait_send()
            joint(part, way).wait_send()
        return 0

    lax.fori_loop(0, PARTS, sent, 0)


def cross(a, b, tables):
    _, (cb, sb), (la, ls), inverse = tables
    vmem = pl.BlockSpec(memory_space=pltpu.VMEM)
    hbm = pl.BlockSpec(memory_space=pl.ANY)
    dma = pltpu.SemaphoreType.DMA
    return pl.pallas_call(
        cross_kernel,
        out_shape=jax.ShapeDtypeStruct((CH, VS // SEG, LAGS), F32),
        in_specs=[hbm, hbm] + [vmem] * 5,
        out_specs=vmem,
        scratch_shapes=[
            pltpu.VMEM((ROWS_MAIN, 2 * NF), F32),
            pltpu.VMEM((ROWS_MAIN, NF + 256), BF),
            pltpu.VMEM((NKB * 16, 2, CH // 8, 8, 128), F32),
            pltpu.VMEM((NC, 2, 2, 4, 4, ROWS_SRC, CL), BF),
            pltpu.VMEM((NKB * 16, VS, 256), BF),
            pltpu.VMEM((2 * NF, CQ * VS), BF),
            pltpu.VMEM((LAGS, 2 * NF), BF),
            pltpu.VMEM((SEG, CH, VS // SEG, LAGS), BF),
            pltpu.VMEM((2, CH, VS // SEG, LAGS), BF),
            pltpu.VMEM((2, PARTS, PC // 2, VS // SEG, LAGS), BF),
            dma((NC * 6,)), dma((NC * 6,)),
            dma((NC * 4,)), dma((NC * 4,)),
            dma((NC * 4,)), dma((NC * 4,)),
            dma((NC * 2,)), dma((NC * 2,)),
            dma((6, PARTS)), dma((6, PARTS)),
            dma((1 + NC * 2,)),
        ],
        compiler_params=pltpu.CompilerParams(
            collective_id=1, has_side_effects=True, vmem_limit_bytes=60 * 1024 * 1024
        ),
        name="cross",
    )(a, b, la, ls, cb, sb, inverse)


def on_device(strain_rate, window_length, source_channel):
    tables = jax.tree.map(jnp.asarray, small_tables())
    a, b = spectra(strain_rate, window_length, source_channel, tables)
    return cross(a, b, tables) * (1.0 / math.sqrt(NF * WIN * SEG))


def solution(mesh):
    in_specs = (P("seg", None, "chan"), P("seg"), P())
    out_specs = P("chan", "seg", None)
    return jax.shard_map(
        on_device, mesh=mesh, in_specs=in_specs, out_specs=out_specs, check_vma=False
    )
```
